768 devices in a mesh: strip: 8 (over y), wide: 48 (over z, x_hi, core), comp: 2 (over x_lo).
Axes of the slice: x: 4 (x_hi: 2, x_lo: 2; x = x_hi * 2 + x_lo), y: 8, z: 12, core: 2. Of those that a mesh axis runs over, the one named last changes fastest.
Arguments:
- spectrum: bfloat16 [1152, 98304], P('comp', ('strip', 'wide')), may hold values from 0.049804688 to 2
- wet_mask: int32 [384, 256], P('strip'), may hold values 0 or 1
- currents: float32 [2, 64, 192], P(None, 'strip', 'wide'), may hold values from -3 to 3
- remap_index: int32 [4, 98304], P(None, 'strip'), may hold values from 0 to 1535, as said below
- remap_weights: float32 [4, 98304], P(None, 'strip'), may hold values from 0.2 to 0.6
- source_matrix: bfloat16 [1152, 1152], P('comp'), may hold values from -0.1875 to 0.1875
Outputs:
- updated: bfloat16 [1152, 98304], P('comp', ('strip', 'wide'))
- stokes: float32 [2, 32, 98304], P(None, 'comp', ('strip', 'wide'))
The draws below stay inside these ranges and needn't reach their ends.
Inputs may be any that keep to these rules, and one draw needn't show every extreme that they name: `remap_index`: a point's cells lie in the ocean rows and columns of its strip next to the point's own location.
All inputs are finite; a program needn't handle non-finite values. No bound on the sum of `wet_mask` on one device may be relied on, other than what follows from the above.
Results may differ from the reference program's by a relative error of at most 0.0048.
Values may be sent and summed in bfloat16 or wider, within the bound.
No kernel may reach another device: no remote copies, remote signals or barrier semaphores. Data moves between devices by JAX's collectives and lax.ppermute only.
A program may use at most 32 MiB of HBM per device.

```python
import math
import jax
import jax.numpy as jnp
from jax import lax

NFREQ = 32
NDIR = 36
LEVELS = 32
LON = 256
SUBSTEPS = 4
LAT_DEV = 48
OLAT_DEV = 8
NBIN = 1152
LAT = 384
NPTS = 98304
OLAT = 64
OLON = 192
N_STRIP = 8


def draw_remap_index(key, part):
    point = jnp.arange(NPTS, dtype=jnp.int32) % (LAT_DEV * LON)
    row = point // LON
    column = point % LON
    span = OLON // LON + 1
    key_row = jax.random.fold_in(key, 11)
    key_column = jax.random.fold_in(key, 23)
    row_shift = jax.random.randint(key_row, (NPTS,), -1, 1, dtype=jnp.int32)
    column_shift = jax.random.randint(key_column, (NPTS,), -1, span, dtype=jnp.int32)
    base_row = jnp.clip(row * OLAT_DEV // LAT_DEV + row_shift, 0, OLAT_DEV - 1)
    base_column = column * OLON // LON + column_shift
    corner = jnp.arange(4, dtype=jnp.int32)
    rows = jnp.minimum(base_row[None, :] + (corner // 2)[:, None], OLAT_DEV - 1)
    columns = (base_column[None, :] + (corner % 2)[:, None] + OLON) % OLON
    return (rows * OLON + columns).astype(jnp.int32)


def set_ends(result, key, least, high):
    longest = result.shape.index(max(result.shape))
    spots = []
    for shift in (0, 1):
        where = [jax.random.randint(jax.random.fold_in(key, axis), (), 0, length) for axis, length in enumerate(result.shape)]
        where[longest] = (where[longest] + shift) % result.shape[longest]
        spots.append(tuple(where))
    return result.at[spots[0]].set(least).at[spots[1]].set(high)


def levels(rng, dims, split, low, top_value):
    loudness, own = 1.0, jax.random.fold_in(rng, 6)
    for dim, shards_of in split:
        heights = jnp.exp(jax.random.uniform(jax.random.fold_in(own, dim), (shards_of,), jnp.float32, low / len(split), top_value / len(split)))
        loudness = loudness * jnp.repeat(heights, dims[dim] // shards_of).reshape([-1 if axis == dim else 1 for axis in range(len(dims))])
    return loudness


def centred(stream_key, extent, scale, most, shards=(), kind=jnp.bfloat16):
    result = scale * jax.random.normal(stream_key, extent, jnp.float32)
    if shards:
        result = result * levels(stream_key, extent, shards, -0.22, 0.18)
    return jnp.clip(result, -most, most).astype(kind)


def setup_inputs(seed: int = 0) -> dict:
    arg_keys = jax.random.split(jax.random.key(seed), 7)
    return {
        "spectrum": jnp.clip(jnp.exp(math.log(2.0) - 3.6927934 * jax.random.uniform(arg_keys[0], (NBIN, NPTS), jnp.float32) ** levels(arg_keys[0], (NBIN, NPTS), ((0, 2), (1, 384)), -0.2, 0.2)), 0.049804688, 2.0).astype(jnp.bfloat16),
        "wet_mask": set_ends((jax.random.randint(arg_keys[1], (LAT, LON), 0, 8) < 7).astype(jnp.int32), jax.random.fold_in(arg_keys[1], 1), 0, 1),
        "currents": centred(arg_keys[2], (2, OLAT, OLON), 0.3, 3.0, ((1, 8), (2, 48)), jnp.float32),
        "remap_index": draw_remap_index(jax.random.fold_in(arg_keys[6], 71), 0),
        "remap_weights": jnp.clip(0.2 + 0.400000021 * jax.random.uniform(arg_keys[4], (4, NPTS), jnp.float32) ** levels(arg_keys[4], (4, NPTS), ((1, 8),), -0.2, 0.2), 0.2, 0.6),
        "source_matrix": centred(arg_keys[5], (NBIN, NBIN), NBIN ** -0.5, 0.1875, ((0, 2),)),
    }


courant = 0.45

def bin_speeds(first_bin, bin_count):
    index = first_bin + jnp.arange(bin_count, dtype=jnp.int32)
    freq_index = (index // NDIR).astype(jnp.float32)
    dir_index = (index % NDIR).astype(jnp.float32)
    group_speed = 0.35 + 0.65 * (NFREQ - 1 - freq_index) / (NFREQ - 1)
    heading = 2.0 * math.pi * (dir_index + 0.5) / NDIR
    return ((group_speed * jnp.cos(heading))[:, None, None], (group_speed * jnp.sin(heading))[:, None, None])

def stokes_kernel(first_bin, bin_count, first_level, level_count):
    index = first_bin + jnp.arange(bin_count, dtype=jnp.int32)
    frequency = (index // NDIR + 1).astype(jnp.float32)
    heading = 2.0 * math.pi * ((index % NDIR).astype(jnp.float32) + 0.5) / NDIR
    level_index = (first_level + jnp.arange(level_count, dtype=jnp.int32)).astype(jnp.float32)
    damping = jnp.exp(-4.0 * frequency[None, :] * (level_index[:, None] + 0.5) / (NFREQ * LEVELS))
    amplitude = damping * (frequency / NFREQ)[None, :] / math.sqrt(NDIR)
    eastward = amplitude * jnp.cos(heading)[None, :]
    northward = amplitude * jnp.sin(heading)[None, :]
    return jnp.concatenate([eastward, northward], 0).astype(jnp.bfloat16)

def substep(energy, east_flow, north_flow, wet_frac, speed_east, speed_north):
    east_speed = speed_east + east_flow[None]
    north_speed = speed_north + north_flow[None]
    flux_lon = jnp.maximum(east_speed, 0.0) * energy + jnp.minimum(jnp.roll(east_speed, -1, 2), 0.0) * jnp.roll(energy, -1, 2)
    flux_lat = jnp.maximum(north_speed[:, :-1], 0.0) * energy[:, :-1] + jnp.minimum(north_speed[:, 1:], 0.0) * energy[:, 1:]
    spread = flux_lon - jnp.roll(flux_lon, 1, 2)
    change = spread[:, 1:-1] + flux_lat[:, 1:] - flux_lat[:, :-1]
    return wet_frac[1:-1] * (energy[:, 1:-1] - courant * change)

def reference(spectrum, wet_mask, currents, remap_index, remap_weights, source_matrix):
    strip_points = LAT_DEV * LON
    ocean_flow = currents.reshape(2, N_STRIP, OLAT_DEV * OLON)
    cell_index = remap_index.reshape(4, N_STRIP, strip_points)
    strip_ids = jnp.arange(N_STRIP, dtype=jnp.int32)[None, :, None]
    picked = ocean_flow[:, strip_ids, cell_index]
    shares = remap_weights.reshape(4, N_STRIP, strip_points)
    surface = lax.optimization_barrier(jnp.sum(picked * shares[None], 1)).reshape(2, LAT, LON)
    wet_frac = wet_mask.astype(jnp.float32)
    padded = jnp.pad(jnp.concatenate([surface, wet_frac[None]], 0), ((0, 0), (1, 1), (0, 0)))
    speed_east, speed_north = bin_speeds(0, NBIN)
    speed_east = speed_east.reshape(NFREQ, NDIR, 1, 1)
    speed_north = speed_north.reshape(NFREQ, NDIR, 1, 1)
    energy = spectrum.astype(jnp.float32).reshape(NFREQ, NDIR, LAT, LON) * wet_frac

    def advect_block(inputs):
        block_energy, block_east, block_north = inputs
        for repeat in range(SUBSTEPS):
            widened = jnp.pad(block_energy, ((0, 0), (1, 1), (0, 0)))
            block_energy = substep(widened, padded[0], padded[1], padded[2], block_east, block_north)
        return block_energy.astype(jnp.bfloat16)
    propagated = lax.map(advect_block, (energy, speed_east, speed_north)).reshape(NBIN, NPTS)
    source = jnp.dot(source_matrix, propagated, preferred_element_type=jnp.float32)
    wet_flat = wet_frac.reshape(-1)
    updated = (wet_flat[None, :] * jnp.maximum(propagated.astype(jnp.float32) + source, 0.0)).astype(jnp.bfloat16)
    kernel = stokes_kernel(0, NBIN, 0, LEVELS)
    stokes = jnp.dot(kernel, propagated, preferred_element_type=jnp.float32).reshape(2, LEVELS, NPTS)
    return (updated, stokes)
```

```python
import math

import jax
import jax.numpy as jnp
from jax import lax
from jax.experimental import pallas as pl
from jax.experimental.pallas import tpu as pltpu
from jax.sharding import PartitionSpec as P

NFREQ = 32
NDIR = 36
LEVELS = 32
SUBSTEPS = 4
OCEAN_ROWS = 8
OCEAN_COLS = 192
ROWS = 4

courant = 0.45


def bin_speeds(first_bin, bin_count):
    index = first_bin + jnp.arange(bin_count, dtype=jnp.int32)
    freq_index = (index // NDIR).astype(jnp.float32)
    dir_index = (index % NDIR).astype(jnp.float32)
    group_speed = 0.35 + 0.65 * (NFREQ - 1 - freq_index) / (NFREQ - 1)
    heading = 2.0 * math.pi * (dir_index + 0.5) / NDIR
    speed_east = courant * group_speed * jnp.cos(heading)
    speed_north = courant * group_speed * jnp.sin(heading)
    return (
        jnp.broadcast_to(speed_east[:, None], (bin_count, 128)),
        jnp.broadcast_to(speed_north[:, None], (bin_count, 128)),
    )


def stokes_kernel(bin_count, first_level, level_count):
    index = jnp.arange(bin_count, dtype=jnp.int32)
    frequency = (index // NDIR + 1).astype(jnp.float32)
    heading = 2.0 * math.pi * ((index % NDIR).astype(jnp.float32) + 0.5) / NDIR
    level_index = (first_level + jnp.arange(level_count, dtype=jnp.int32)).astype(jnp.float32)
    damping = jnp.exp(-4.0 * frequency[None, :] * (level_index[:, None] + 0.5) / (NFREQ * LEVELS))
    amplitude = damping * (frequency / NFREQ)[None, :] / math.sqrt(NDIR)
    eastward = amplitude * jnp.cos(heading)[None, :]
    northward = amplitude * jnp.sin(heading)[None, :]
    return jnp.concatenate([eastward, northward], 0).astype(jnp.bfloat16)


def interpolate_body(table_ref, index_ref, weight_ref, mask_ref, out_ref):
    rows, cols = mask_ref.shape
    row_ids = lax.broadcasted_iota(jnp.int32, (OCEAN_ROWS, 128), 0)
    tables = [table_ref[q] for q in range(4)]
    for chunk in range(rows * cols // 128):
        lanes = slice(chunk * 128, chunk * 128 + 128)
        cells = index_ref[:, lanes]
        shares = weight_ref[:, lanes]
        row_of = (cells * 5462) >> 20
        column_of = cells - row_of * OCEAN_COLS
        lane_of = (column_of >> 4) * 8 + (column_of & 3)
        quarter_of = (column_of >> 2) & 3
        totals = [jnp.zeros((OCEAN_ROWS, 128), jnp.float32) for _ in range(2)]
        for corner in range(4):
            row_b = jnp.broadcast_to(row_of[corner : corner + 1], (OCEAN_ROWS, 128))
            lane_b = jnp.broadcast_to(lane_of[corner : corner + 1], (OCEAN_ROWS, 128))
            quarter_b = jnp.broadcast_to(quarter_of[corner : corner + 1], (OCEAN_ROWS, 128))
            share_b = jnp.broadcast_to(shares[corner : corner + 1], (OCEAN_ROWS, 128))
            weight = jnp.where(row_b == row_ids, share_b, 0.0)
            for c in range(2):
                picked = jnp.take_along_axis(tables[0], lane_b + 4 * c, axis=1)
                for q in range(1, 4):
                    other = jnp.take_along_axis(tables[q], lane_b + 4 * c, axis=1)
                    picked = jnp.where(quarter_b == q, other, picked)
                totals[c] += picked * weight
        row = chunk * 128 // cols
        spot = slice(chunk * 128 % cols, chunk * 128 % cols + 128)
        for c in range(2):
            out_ref[c * rows + row : c * rows + row + 1, spot] = courant * jnp.sum(
                totals[c], axis=0, keepdims=True
            )
    out_ref[2 * rows : 3 * rows, :] = mask_ref[...].astype(jnp.float32)
    out_ref[3 * rows :, :] = jnp.zeros((rows, cols), jnp.float32)


def interpolate(table, cells, shares, mask):
    rows, cols = mask.shape
    return pl.pallas_call(
        interpolate_body,
        out_shape=jax.ShapeDtypeStruct((4 * rows, cols), jnp.float32),
        in_specs=[pl.BlockSpec(memory_space=pltpu.VMEM)] * 4,
        out_specs=pl.BlockSpec(memory_space=pltpu.VMEM),
        cost_estimate=pl.CostEstimate(flops=2_000_000, bytes_accessed=100_000, transcendentals=0),
        name="interpolate",
    )(table, cells, shares, mask)


def propagate_body(
    below_ref, own_ref, above_ref, fbelow_ref, fown_ref, fabove_ref, east_ref, north_ref, out_ref
):
    rows, bins, cols = own_ref.shape
    tile = 16

    def one_tile(t, carry):
        spot = pl.ds(pl.multiple_of(t * tile, tile), tile)
        speed_east = jnp.concatenate([east_ref[spot, :]] * (cols // 128), 1)
        speed_north = jnp.concatenate([north_ref[spot, :]] * (cols // 128), 1)
        energy, masks = [], []
        coefs = []
        for source, fields in ((below_ref, fbelow_ref), (own_ref, fown_ref), (above_ref, fabove_ref)):
            for row in range(rows):
                mask = fields[2 * rows + row : 2 * rows + row + 1, :]
                east = speed_east + fields[row : row + 1, :]
                north = speed_north + fields[rows + row : rows + row + 1, :]
                to_east = jnp.maximum(east, 0.0)
                to_north = jnp.maximum(north, 0.0)
                stay = (1.0 - jnp.abs(east)) - jnp.abs(north)
                coefs.append((stay, to_east, to_east - east, to_north, to_north - north))
                energy.append(source[row, spot, :].astype(jnp.float32) * mask)
                masks.append(mask)
        count = 3 * rows
        for step in range(SUBSTEPS):
            low, high = step + 1, count - 1 - step
            fresh = list(energy)
            for i in range(low, high):
                stay, to_east, to_west, _, _ = coefs[i]
                moved = stay * energy[i]
                moved += pltpu.roll(to_east * energy[i], 1, 1)
                moved += pltpu.roll(to_west * energy[i], cols - 1, 1)
                moved += coefs[i - 1][3] * energy[i - 1]
                moved += coefs[i + 1][4] * energy[i + 1]
                fresh[i] = moved * masks[i]
            energy = fresh
        for row in range(rows):
            result = energy[rows + row].astype(jnp.bfloat16)
            out_ref[row, spot, :] = result
            out_ref[rows + row, spot, :] = result
        return carry

    lax.fori_loop(0, bins // tile, one_tile, 0)


def propagate(below, own, above, fbelow, fown, fabove, east, north):
    rows, bins, cols = own.shape
    return pl.pallas_call(
        propagate_body,
        out_shape=jax.ShapeDtypeStruct((2 * rows, bins, cols), jnp.bfloat16),
        in_specs=[pl.BlockSpec(memory_space=pltpu.VMEM)] * 8,
        out_specs=pl.BlockSpec(memory_space=pltpu.VMEM),
        cost_estimate=pl.CostEstimate(flops=40_000_000, bytes_accessed=1_600_000, transcendentals=0),
        name="propagate",
    )(below, own, above, fbelow, fown, fabove, east, north)


def per_device(spectrum, wet_mask, currents, remap_index, remap_weights, source_matrix):
    wide_index = lax.axis_index("wide")
    comp_index = lax.axis_index("comp")
    strips, wides = lax.axis_size("strip"), lax.axis_size("wide")
    comps = lax.axis_size("comp")
    lat_rows, lon_cells = wet_mask.shape
    local_bins, points = spectrum.shape
    groups = wides // ROWS
    group_index = wide_index // ROWS
    member = wide_index % ROWS
    share = local_bins // ROWS
    near = [[ROWS * g + i for i in range(ROWS)] for g in range(groups)]
    far = [[ROWS * g + i for g in range(groups)] for i in range(ROWS)]

    lane = jnp.arange(128, dtype=jnp.int32)
    ours = jnp.concatenate([currents[0], currents[1]], axis=1)
    ours = jnp.where((lane // 8 == group_index)[None, :], jnp.tile(ours, (1, 16)), 0.0)
    along = lax.all_to_all(
        jnp.broadcast_to(ours[None], (groups, OCEAN_ROWS, 128)),
        "wide", split_axis=0, concat_axis=0, tiled=True, axis_index_groups=far,
    )
    along = jnp.sum(along, 0)
    table = lax.all_to_all(
        jnp.broadcast_to(along[None], (ROWS, OCEAN_ROWS, 128)),
        "wide", split_axis=0, concat_axis=0, tiled=True, axis_index_groups=near,
    )

    own = lax.all_to_all(
        spectrum.reshape(ROWS, share, points),
        "wide", split_axis=0, concat_axis=0, tiled=True, axis_index_groups=near,
    )
    total = strips * wides
    upward = [(i, i + ROWS) for i in range(total - ROWS)]
    downward = [(i + ROWS, i) for i in range(total - ROWS)]
    chain = ("strip", "wide")
    below = lax.ppermute(own, chain, upward)
    above = lax.ppermute(own, chain, downward)

    first = group_index * ROWS * lon_cells
    cells = lax.dynamic_slice_in_dim(remap_index, first, ROWS * lon_cells, 1)
    shares = lax.dynamic_slice_in_dim(remap_weights, first, ROWS * lon_cells, 1)
    mask = lax.dynamic_slice_in_dim(wet_mask, group_index * ROWS, ROWS, 0)
    fown = interpolate(table, cells, shares, mask)
    fbelow = lax.ppermute(fown, chain, upward)
    fabove = lax.ppermute(fown, chain, downward)

    first_bin = comp_index * local_bins + member * share
    east, north = bin_speeds(first_bin, share)
    spread = propagate(below, own, above, fbelow, fown, fabove, east, north)

    both = [
        [(ROWS * g + i) * comps + k for k in range(comps) for i in range(ROWS)] for g in range(groups)
    ]
    fragment = lax.all_to_all(
        spread, ("wide", "comp"), split_axis=0, concat_axis=0, tiled=True, axis_index_groups=both
    ).reshape(comps * local_bins, points)

    level_rows = LEVELS // comps
    kernel = stokes_kernel(comps * local_bins, comp_index * level_rows, level_rows)
    source_part = jnp.dot(source_matrix, fragment, preferred_element_type=jnp.float32)
    drift_part = jnp.dot(kernel, fragment, preferred_element_type=jnp.float32)
    returned = lax.dynamic_slice_in_dim(fragment, comp_index * local_bins, local_bins, 0)
    wet_points = lax.dynamic_slice_in_dim(wet_mask, wide_index, 1, 0).astype(jnp.float32)
    updated = (
        wet_points * jnp.maximum(returned.astype(jnp.float32) + source_part, 0.0)
    ).astype(jnp.bfloat16)
    return (updated, drift_part.reshape(2, level_rows, points))


def solution(mesh):
    placed = (
        P("comp", ("strip", "wide")),
        P("strip", None),
        P(None, "strip", "wide"),
        P(None, "strip"),
        P(None, "strip"),
        P("comp", None),
    )
    return jax.shard_map(
        per_device,
        mesh=mesh,
        in_specs=placed,
        out_specs=(P("comp", ("strip", "wide")), P(None, "comp", ("strip", "wide"))),
        check_vma=False,
    )
```

```python
import math

import jax
import jax.numpy as jnp
from jax import lax
from jax.experimental import pallas as pl
from jax.experimental.pallas import tpu as pltpu
from jax.sharding import PartitionSpec as P


NFREQ = 32
NDIR = 36
LEVELS = 32
SUBSTEPS = 4
OCEAN_ROWS = 8
OCEAN_COLS = 192
ROWS = 4

courant = 0.45


def bin_speeds(first_bin, bin_count):
    index = first_bin + jnp.arange(bin_count, dtype=jnp.int32)
    freq_index = (index // NDIR).astype(jnp.float32)
    dir_index = (index % NDIR).astype(jnp.float32)
    group_speed = 0.35 + 0.65 * (NFREQ - 1 - freq_index) / (NFREQ - 1)
    heading = 2.0 * math.pi * (dir_index + 0.5) / NDIR
    speed_east = courant * group_speed * jnp.cos(heading)
    speed_north = courant * group_speed * jnp.sin(heading)
    return (
        jnp.broadcast_to(speed_east[:, None], (bin_count, 128)),
        jnp.broadcast_to(speed_north[:, None], (bin_count, 128)),
    )


def stokes_kernel(bin_count, first_level, level_count):
    index = jnp.arange(bin_count, dtype=jnp.int32)
    frequency = (index // NDIR + 1).astype(jnp.float32)
    heading = 2.0 * math.pi * ((index % NDIR).astype(jnp.float32) + 0.5) / NDIR
    level_index = (first_level + jnp.arange(level_count, dtype=jnp.int32)).astype(jnp.float32)
    damping = jnp.exp(-4.0 * frequency[None, :] * (level_index[:, None] + 0.5) / (NFREQ * LEVELS))
    amplitude = damping * (frequency / NFREQ)[None, :] / math.sqrt(NDIR)
    eastward = amplitude * jnp.cos(heading)[None, :]
    northward = amplitude * jnp.sin(heading)[None, :]
    return jnp.concatenate([eastward, northward], 0).astype(jnp.bfloat16)


def interpolate_body(
    place_ref, gathered_ref, index_ref, weight_ref, mask_ref, out_ref
):
    groups = gathered_ref.shape[0]
    cols = mask_ref.shape[1]
    rows = ROWS
    row_ids = lax.broadcasted_iota(jnp.int32, (OCEAN_ROWS, 128), 0)
    tables = []
    for part in range(groups // 4):
        pieces = [gathered_ref[4 * part + i] for i in range(4)]
        tables.append((pieces[0] + pieces[1]) + (pieces[2] + pieces[3]))
    for chunk in range(rows * cols // 128):
        lanes = slice(chunk * 128, chunk * 128 + 128)
        cells = index_ref[:, lanes]
        shares = weight_ref[:, lanes]
        row_of = (cells * 5462) >> 20
        column_of = cells - row_of * OCEAN_COLS
        lane_of = ((column_of & 63) >> 2) * 8 + (column_of & 3)
        part_of = column_of >> 6
        totals = [jnp.zeros((OCEAN_ROWS, 128), jnp.float32) for _ in range(2)]
        for corner in range(4):
            row_b = jnp.broadcast_to(row_of[corner : corner + 1], (OCEAN_ROWS, 128))
            lane_b = jnp.broadcast_to(lane_of[corner : corner + 1], (OCEAN_ROWS, 128))
            part_b = jnp.broadcast_to(part_of[corner : corner + 1], (OCEAN_ROWS, 128))
            share_b = jnp.broadcast_to(shares[corner : corner + 1], (OCEAN_ROWS, 128))
            weight = jnp.where(row_b == row_ids, share_b, 0.0)
            for c in range(2):
                picked = jnp.take_along_axis(tables[0], lane_b + 4 * c, axis=1)
                for part in range(1, len(tables)):
                    other = jnp.take_along_axis(tables[part], lane_b + 4 * c, axis=1)
                    picked = jnp.where(part_b == part, other, picked)
                totals[c] += picked * weight
        row = chunk * 128 // cols
        spot = slice(chunk * 128 % cols, chunk * 128 % cols + 128)
        for c in range(2):
            out_ref[c * rows + row : c * rows + row + 1, spot] = courant * jnp.sum(
                totals[c], axis=0, keepdims=True
            )
    upper = place_ref[pl.program_id(0)] % 2 == 1
    mask = jnp.where(upper, mask_ref[rows : 2 * rows, :], mask_ref[0:rows, :])
    out_ref[2 * rows : 3 * rows, :] = mask.astype(jnp.float32)
    out_ref[3 * rows :, :] = jnp.zeros((rows, cols), jnp.float32)


def interpolate(places, gathered, remap_index, remap_weights, wet_mask):
    count = places.shape[0]
    cols = wet_mask.shape[1]
    block = ROWS * cols
    return pl.pallas_call(
        interpolate_body,
        grid_spec=pltpu.PrefetchScalarGridSpec(
            num_scalar_prefetch=1,
            grid=(count,),
            in_specs=[
                pl.BlockSpec(gathered.shape, lambda i, place: (0, 0, 0)),
                pl.BlockSpec((4, block), lambda i, place: (0, place[i])),
                pl.BlockSpec((4, block), lambda i, place: (0, place[i])),
                pl.BlockSpec((2 * ROWS, cols), lambda i, place: (place[i] // 2, 0)),
            ],
            out_specs=pl.BlockSpec((4 * ROWS, cols), lambda i, place: (i, 0)),
        ),
        out_shape=jax.ShapeDtypeStruct((count * 4 * ROWS, cols), jnp.float32),
        compiler_params=pltpu.CompilerParams(vmem_limit_bytes=4 << 20),
        cost_estimate=pl.CostEstimate(
            flops=2_000_000 * count, bytes_accessed=100_000 * count, transcendentals=0
        ),
        name="interpolate",
    )(places, gathered, remap_index, remap_weights, wet_mask)


def propagate_body(
    edge_ref, below_ref, own_ref, above_ref, fown_ref, fbeside_ref, fother_ref, east_ref, north_ref,
    out_ref, fbelow_ref, fabove_ref,
):
    rows, bins, cols = own_ref.shape
    tile = 16
    deep = 4 * rows
    fother = fother_ref[...]
    fbelow_ref[...] = jnp.where(edge_ref[0] == 1, fother, fbeside_ref[0:deep, :])
    fabove_ref[...] = jnp.where(edge_ref[1] == 1, fother, fbeside_ref[deep:, :])

    def one_tile(t, carry):
        spot = pl.ds(pl.multiple_of(t * tile, tile), tile)
        speed_east = jnp.concatenate([east_ref[spot, :]] * (cols // 128), 1)
        speed_north = jnp.concatenate([north_ref[spot, :]] * (cols // 128), 1)
        energy, masks = [], []
        coefs = []
        for source, fields in ((below_ref, fbelow_ref), (own_ref, fown_ref), (above_ref, fabove_ref)):
            for row in range(rows):
                mask = fields[2 * rows + row : 2 * rows + row + 1, :]
                east = speed_east + fields[row : row + 1, :]
                north = speed_north + fields[rows + row : rows + row + 1, :]
                to_east = jnp.maximum(east, 0.0)
                to_north = jnp.maximum(north, 0.0)
                stay = (1.0 - jnp.abs(east)) - jnp.abs(north)
                coefs.append((stay, to_east, to_east - east, to_north, to_north - north))
                energy.append(source[row, spot, :].astype(jnp.float32) * mask)
                masks.append(mask)
        count = 3 * rows
        for step in range(SUBSTEPS):
            low, high = step + 1, count - 1 - step
            fresh = list(energy)
            for i in range(low, high):
                stay, to_east, to_west, _, _ = coefs[i]
                moved = stay * energy[i]
                moved += pltpu.roll(to_east * energy[i], 1, 1)
                moved += pltpu.roll(to_west * energy[i], cols - 1, 1)
                moved += coefs[i - 1][3] * energy[i - 1]
                moved += coefs[i + 1][4] * energy[i + 1]
                fresh[i] = moved * masks[i]
            energy = fresh
        for row in range(rows):
            result = energy[rows + row].astype(jnp.bfloat16)
            out_ref[row, spot, :] = result
            out_ref[rows + row, spot, :] = result
        return carry

    lax.fori_loop(0, bins // tile, one_tile, 0)


def propagate(edges, below, own, above, fown, fbeside, fother, east, north):
    rows, bins, cols = own.shape
    return pl.pallas_call(
        propagate_body,
        out_shape=jax.ShapeDtypeStruct((2 * rows, bins, cols), jnp.bfloat16),
        in_specs=[pl.BlockSpec(memory_space=pltpu.SMEM)]
        + [pl.BlockSpec(memory_space=pltpu.VMEM)] * 8,
        out_specs=pl.BlockSpec(memory_space=pltpu.VMEM),
        scratch_shapes=[pltpu.VMEM((4 * rows, cols), jnp.float32)] * 2,
        compiler_params=pltpu.CompilerParams(vmem_limit_bytes=8 << 20),
        cost_estimate=pl.CostEstimate(flops=40_000_000, bytes_accessed=1_600_000, transcendentals=0),
        name="propagate",
    )(edges, below, own, above, fown, fbeside, fother, east, north)


def step(spectrum, wet_mask, currents, remap_index, remap_weights, source_matrix):
    wide_index = lax.axis_index("wide")
    comp_index = lax.axis_index("comp")
    strips, wides = lax.axis_size("strip"), lax.axis_size("wide")
    comps = lax.axis_size("comp")
    local_bins, points = spectrum.shape
    groups = wides // ROWS
    group_index = wide_index // ROWS
    member = wide_index % ROWS
    share = local_bins // ROWS
    near = [[ROWS * g + i for i in range(ROWS)] for g in range(groups)]
    far = [[ROWS * g + i for g in range(groups)] for i in range(ROWS)]

    lane = jnp.arange(128, dtype=jnp.int32)
    ours = jnp.concatenate([currents[0], currents[1]], axis=1)
    ours = jnp.where((lane // 8 == wide_index % 16)[None, :], jnp.tile(ours, (1, 16)), 0.0)
    table = ours
    for turn in range(1, ROWS):
        swap = [(i, i - i % ROWS + (i % ROWS ^ turn)) for i in range(wides)]
        table = table + lax.ppermute(ours, "wide", swap)
    own = lax.all_to_all(
        spectrum.reshape(ROWS, share, points),
        "wide", split_axis=0, concat_axis=0, tiled=True, axis_index_groups=near,
    )
    table = lax.all_to_all(
        jnp.broadcast_to(table[None], (groups, OCEAN_ROWS, 128)),
        "wide", split_axis=0, concat_axis=0, tiled=True, axis_index_groups=far,
    )
    total = strips * wides
    upward = [(i, i + ROWS) for i in range(total - ROWS)]
    downward = [(i + ROWS, i) for i in range(total - ROWS)]
    chain = ("strip", "wide")
    below = lax.ppermute(own, chain, upward)
    above = lax.ppermute(own, chain, downward)
    args = (table, remap_index, remap_weights, wet_mask)
    fown = interpolate(group_index.reshape(1), *args)
    crossing = [(s * wides + wides - ROWS + i, (s + 1) * wides + i) for s in range(strips - 1) for i in range(ROWS)]
    fother = lax.ppermute(fown, chain, crossing + [(b, a) for a, b in crossing])
    beside = jnp.stack([jnp.maximum(group_index - 1, 0), jnp.minimum(group_index + 1, groups - 1)])
    fbeside = interpolate(beside, *args)
    edges = jnp.stack([group_index == 0, group_index == groups - 1]).astype(jnp.int32)

    first_bin = comp_index * local_bins + member * share
    east, north = bin_speeds(first_bin, share)
    spread = propagate(edges, below, own, above, fown, fbeside, fother, east, north)

    both = [
        [(ROWS * g + i) * comps + k for k in range(comps) for i in range(ROWS)] for g in range(groups)
    ]
    fragment = lax.all_to_all(
        spread, ("wide", "comp"), split_axis=0, concat_axis=0, tiled=True, axis_index_groups=both
    ).reshape(comps * local_bins, points)

    level_rows = LEVELS // comps
    kernel = stokes_kernel(comps * local_bins, comp_index * level_rows, level_rows)
    source_part = jnp.dot(source_matrix, fragment, preferred_element_type=jnp.float32)
    drift_part = jnp.dot(kernel, fragment, preferred_element_type=jnp.float32)
    returned = lax.dynamic_slice_in_dim(fragment, comp_index * local_bins, local_bins, 0)
    wet_points = lax.dynamic_slice_in_dim(wet_mask, wide_index, 1, 0).astype(jnp.float32)
    updated = (
        wet_points * jnp.maximum(returned.astype(jnp.float32) + source_part, 0.0)
    ).astype(jnp.bfloat16)
    return (updated, drift_part.reshape(2, level_rows, points))


def solution(mesh):
    placed = (
        P("comp", ("strip", "wide")),
        P("strip", None),
        P(None, "strip", "wide"),
        P(None, "strip"),
        P(None, "strip"),
        P("comp", None),
    )
    return jax.shard_map(
        step,
        mesh=mesh,
        in_specs=placed,
        out_specs=(P("comp", ("strip", "wide")), P(None, "comp", ("strip", "wide"))),
        check_vma=False,
    )
```

```python
import functools
import math

import jax
import jax.numpy as jnp
from jax import lax
from jax.experimental import pallas as pl
from jax.experimental.pallas import tpu as pltpu
from jax.sharding import PartitionSpec as P


NFREQ = 32
NDIR = 36
LEVELS = 32
SUBSTEPS = 4
OCEAN_ROWS = 8
OCEAN_COLS = 192
EXTRA = 16
ROWS = 4

courant = 0.45


def bin_speeds(first_bin, bin_count):
    index = first_bin + jnp.arange(bin_count, dtype=jnp.int32)
    freq_index = (index // NDIR).astype(jnp.float32)
    dir_index = (index % NDIR).astype(jnp.float32)
    group_speed = 0.35 + 0.65 * (NFREQ - 1 - freq_index) / (NFREQ - 1)
    heading = 2.0 * math.pi * (dir_index + 0.5) / NDIR
    speed_east = courant * group_speed * jnp.cos(heading)
    speed_north = courant * group_speed * jnp.sin(heading)
    return (
        jnp.broadcast_to(speed_east[:, None], (bin_count, 128)),
        jnp.broadcast_to(speed_north[:, None], (bin_count, 128)),
    )


def stokes_kernel(bin_count, first_level, level_count):
    index = jnp.arange(bin_count, dtype=jnp.int32)
    frequency = (index // NDIR + 1).astype(jnp.float32)
    heading = 2.0 * math.pi * ((index % NDIR).astype(jnp.float32) + 0.5) / NDIR
    level_index = (first_level + jnp.arange(level_count, dtype=jnp.int32)).astype(jnp.float32)
    damping = jnp.exp(-4.0 * frequency[None, :] * (level_index[:, None] + 0.5) / (NFREQ * LEVELS))
    amplitude = damping * (frequency / NFREQ)[None, :] / math.sqrt(NDIR)
    eastward = amplitude * jnp.cos(heading)[None, :]
    northward = amplitude * jnp.sin(heading)[None, :]
    return jnp.concatenate([eastward, northward], 0).astype(jnp.bfloat16)


def pack_body(place_ref, spectrum_ref, currents_ref, out_ref, done):
    members, bins, _ = spectrum_ref.shape
    copy = pltpu.make_async_copy(spectrum_ref, out_ref.at[:, pl.ds(0, bins), :], done)
    copy.start()
    lane = lax.broadcasted_iota(jnp.int32, (OCEAN_ROWS, 128), 1)
    ours = jnp.zeros((OCEAN_ROWS, 128), jnp.float32)
    for c in range(2):
        for i in range(4):
            column = jnp.broadcast_to(currents_ref[c, :, i : i + 1], (OCEAN_ROWS, 128))
            ours = jnp.where((lane & 7) == 4 * c + i, column, ours)
    ours = jnp.where((lane >> 3) == place_ref[0], ours, 0.0)
    high = ours.astype(jnp.bfloat16).astype(jnp.float32)
    rest = ours - high
    middle = rest.astype(jnp.bfloat16).astype(jnp.float32)
    low = rest - middle
    block = jnp.concatenate(
        [jnp.concatenate([high, middle], 1), jnp.concatenate([low, jnp.zeros_like(low)], 1)], 0
    ).astype(jnp.bfloat16)
    for member in range(members):
        out_ref[member, bins:, :] = block
    copy.wait()


def pack(place, spectrum, currents):
    members, bins, cols = spectrum.shape
    return pl.pallas_call(
        pack_body,
        out_shape=jax.ShapeDtypeStruct((members, bins + EXTRA, cols), jnp.bfloat16),
        in_specs=[
            pl.BlockSpec(memory_space=pltpu.SMEM),
            pl.BlockSpec(memory_space=pl.ANY),
            pl.BlockSpec(memory_space=pltpu.VMEM),
        ],
        out_specs=pl.BlockSpec(memory_space=pltpu.VMEM),
        scratch_shapes=[pltpu.SemaphoreType.DMA],
        compiler_params=pltpu.CompilerParams(vmem_limit_bytes=4 << 20),
        cost_estimate=pl.CostEstimate(flops=100_000, bytes_accessed=700_000, transcendentals=0),
        name="pack",
    )(place, spectrum, currents)


def unpack_body(own_ref, out_ref):
    members = own_ref.shape[0]
    table = jnp.zeros((OCEAN_ROWS, 128), jnp.float32)
    for member in range(members):
        block = own_ref[member].astype(jnp.float32)
        upper, lower = block[:OCEAN_ROWS], block[OCEAN_ROWS:]
        table += (upper[:, :128] + upper[:, 128:]) + lower[:, :128]
    for group in range(out_ref.shape[0]):
        out_ref[group] = table


def unpack(own, groups):
    members, depth, cols = own.shape
    return pl.pallas_call(
        unpack_body,
        grid=(1,),
        out_shape=jax.ShapeDtypeStruct((groups, OCEAN_ROWS, 128), jnp.float32),
        in_specs=[pl.BlockSpec((members, EXTRA, cols), lambda i: (0, depth // EXTRA - 1, 0))],
        out_specs=pl.BlockSpec((groups, OCEAN_ROWS, 128), lambda i: (0, 0, 0)),
        compiler_params=pltpu.CompilerParams(vmem_limit_bytes=4 << 20),
        cost_estimate=pl.CostEstimate(flops=20_000, bytes_accessed=100_000, transcendentals=0),
        name="unpack",
    )(own)


def fetch_body(place_ref, index_ref, weight_ref, mask_ref, code_ref, share_ref, wet_ref):
    cells = index_ref[...]
    row_of = (cells * 5462) >> 20
    column_of = cells - row_of * OCEAN_COLS
    lane_of = ((column_of & 63) >> 2) * 8 + (column_of & 3)
    code_ref[0] = row_of * 1024 + (column_of >> 6) * 128 + lane_of
    share_ref[0] = weight_ref[...]
    upper = place_ref[pl.program_id(0)] % 2 == 1
    mask = jnp.where(upper, mask_ref[ROWS:, :], mask_ref[:ROWS, :])
    wet_ref[0] = mask.astype(jnp.float32)


def fetch(places, remap_index, remap_weights, wet_mask):
    count = places.shape[0]
    cols = wet_mask.shape[1]
    block = ROWS * cols
    return pl.pallas_call(
        fetch_body,
        grid_spec=pltpu.PrefetchScalarGridSpec(
            num_scalar_prefetch=1,
            grid=(count,),
            in_specs=[
                pl.BlockSpec((4, block), lambda i, place: (0, place[i])),
                pl.BlockSpec((4, block), lambda i, place: (0, place[i])),
                pl.BlockSpec((2 * ROWS, cols), lambda i, place: (place[i] // 2, 0)),
            ],
            out_specs=[
                pl.BlockSpec((1, 4, block), lambda i, place: (i, 0, 0)),
                pl.BlockSpec((1, 4, block), lambda i, place: (i, 0, 0)),
                pl.BlockSpec((1, ROWS, cols), lambda i, place: (i, 0, 0)),
            ],
        ),
        out_shape=[
            jax.ShapeDtypeStruct((count, 4, block), jnp.int32),
            jax.ShapeDtypeStruct((count, 4, block), jnp.float32),
            jax.ShapeDtypeStruct((count, ROWS, cols), jnp.float32),
        ],
        compiler_params=pltpu.CompilerParams(vmem_limit_bytes=4 << 20),
        cost_estimate=pl.CostEstimate(flops=100_000, bytes_accessed=300_000, transcendentals=0),
        name="fetch",
    )(places, remap_index, remap_weights, wet_mask)


def interpolate_body(blocks, gathered_ref, code_ref, share_ref, wet_ref, out_ref):
    groups = gathered_ref.shape[0]
    rows, cols = wet_ref.shape[1:]
    row_ids = lax.broadcasted_iota(jnp.int32, (OCEAN_ROWS, 128), 0)
    tables = []
    for part in range(groups // 4):
        pieces = [gathered_ref[4 * part + i] for i in range(4)]
        tables.append((pieces[0] + pieces[1]) + (pieces[2] + pieces[3]))
    for place, block in enumerate(blocks):
        base = place * 4 * rows
        for chunk in range(rows * cols // 128):
            lanes = slice(chunk * 128, chunk * 128 + 128)
            codes = code_ref[block, :, lanes]
            shares = share_ref[block, :, lanes]
            totals = [jnp.zeros((OCEAN_ROWS, 128), jnp.float32) for _ in range(2)]
            for corner in range(4):
                code_b = jnp.broadcast_to(codes[corner : corner + 1], (OCEAN_ROWS, 128))
                share_b = jnp.broadcast_to(shares[corner : corner + 1], (OCEAN_ROWS, 128))
                part_b = (code_b >> 7) & 7
                weight = jnp.where((code_b >> 10) == row_ids, share_b, 0.0)
                for c in range(2):
                    lane_b = (code_b & 127) + 4 * c
                    picked = jnp.take_along_axis(tables[0], lane_b, axis=1)
                    for part in range(1, len(tables)):
                        other = jnp.take_along_axis(tables[part], lane_b, axis=1)
                        picked = jnp.where(part_b == part, other, picked)
                    totals[c] += picked * weight
            row = chunk * 128 // cols
            spot = slice(chunk * 128 % cols, chunk * 128 % cols + 128)
            for c in range(2):
                at = base + c * rows + row
                out_ref[at : at + 1, spot] = courant * jnp.sum(totals[c], axis=0, keepdims=True)
        out_ref[base + 2 * rows : base + 3 * rows, :] = wet_ref[block]
        out_ref[base + 3 * rows : base + 4 * rows, :] = jnp.zeros((rows, cols), jnp.float32)


def interpolate(blocks, gathered, codes, shares, wet):
    count = len(blocks)
    rows, cols = wet.shape[1:]
    return pl.pallas_call(
        functools.partial(interpolate_body, blocks),
        out_shape=jax.ShapeDtypeStruct((count * 4 * rows, cols), jnp.float32),
        in_specs=[pl.BlockSpec(memory_space=pltpu.VMEM)] * 4,
        out_specs=pl.BlockSpec(memory_space=pltpu.VMEM),
        compiler_params=pltpu.CompilerParams(vmem_limit_bytes=4 << 20),
        cost_estimate=pl.CostEstimate(
            flops=2_000_000 * count, bytes_accessed=100_000 * count, transcendentals=0
        ),
        name="interpolate",
    )(gathered, codes, shares, wet)


def propagate_body(
    edge_ref, below_ref, own_ref, above_ref, fown_ref, fbeside_ref, fother_ref, east_ref, north_ref,
    out_ref, fbelow_ref, fabove_ref,
):
    rows, bins, cols = below_ref.shape
    tile = 16
    deep = 4 * rows
    fother = fother_ref[...]
    fbelow_ref[...] = jnp.where(edge_ref[0] == 1, fother, fbeside_ref[0:deep, :])
    fabove_ref[...] = jnp.where(edge_ref[1] == 1, fother, fbeside_ref[deep:, :])

    def one_tile(t, carry):
        spot = pl.ds(pl.multiple_of(t * tile, tile), tile)
        speed_east = jnp.concatenate([east_ref[spot, :]] * (cols // 128), 1)
        speed_north = jnp.concatenate([north_ref[spot, :]] * (cols // 128), 1)
        energy, masks = [], []
        coefs = []
        for source, fields in ((below_ref, fbelow_ref), (own_ref, fown_ref), (above_ref, fabove_ref)):
            for row in range(rows):
                mask = fields[2 * rows + row : 2 * rows + row + 1, :]
                east = speed_east + fields[row : row + 1, :]
                north = speed_north + fields[rows + row : rows + row + 1, :]
                to_east = jnp.maximum(east, 0.0)
                to_north = jnp.maximum(north, 0.0)
                stay = (1.0 - jnp.abs(east)) - jnp.abs(north)
                coefs.append((stay, to_east, to_east - east, to_north, to_north - north))
                energy.append(source[row, spot, :].astype(jnp.float32) * mask)
                masks.append(mask)
        count = 3 * rows
        for step in range(SUBSTEPS):
            low, high = step + 1, count - 1 - step
            fresh = list(energy)
            for i in range(low, high):
                stay, to_east, to_west, _, _ = coefs[i]
                moved = stay * energy[i]
                moved += pltpu.roll(to_east * energy[i], 1, 1)
                moved += pltpu.roll(to_west * energy[i], cols - 1, 1)
                moved += coefs[i - 1][3] * energy[i - 1]
                moved += coefs[i + 1][4] * energy[i + 1]
                fresh[i] = moved * masks[i]
            energy = fresh
        for row in range(rows):
            result = energy[rows + row].astype(jnp.bfloat16)
            out_ref[row, spot, :] = result
            out_ref[rows + row, spot, :] = result
        return carry

    lax.fori_loop(0, bins // tile, one_tile, 0)


def propagate(edges, below, own, above, fown, fbeside, fother, east, north):
    rows, bins, cols = below.shape
    return pl.pallas_call(
        propagate_body,
        out_shape=jax.ShapeDtypeStruct((2 * rows, bins, cols), jnp.bfloat16),
        in_specs=[pl.BlockSpec(memory_space=pltpu.SMEM)]
        + [pl.BlockSpec(memory_space=pltpu.VMEM)] * 8,
        out_specs=pl.BlockSpec(memory_space=pltpu.VMEM),
        scratch_shapes=[pltpu.VMEM((4 * rows, cols), jnp.float32)] * 2,
        compiler_params=pltpu.CompilerParams(vmem_limit_bytes=8 << 20),
        cost_estimate=pl.CostEstimate(flops=40_000_000, bytes_accessed=1_600_000, transcendentals=0),
        name="propagate",
    )(edges, below, own, above, fown, fbeside, fother, east, north)


def finish_body(comp_ref, fragment_ref, source_ref, kernel_ref, wet_ref, updated_ref, stokes_ref):
    rows = updated_ref.shape[0]
    steps = pl.num_programs(0)
    fragment = fragment_ref[...]
    source = jnp.dot(source_ref[...], fragment, preferred_element_type=jnp.float32)
    first = (comp_ref[0] * steps + pl.program_id(0)) * rows
    returned = fragment_ref[pl.ds(pl.multiple_of(first, 16), rows), :].astype(jnp.float32)
    updated_ref[...] = (wet_ref[...] * jnp.maximum(returned + source, 0.0)).astype(jnp.bfloat16)

    @pl.when(pl.program_id(0) == 0)
    def _():
        stokes_ref[...] = jnp.dot(kernel_ref[...], fragment, preferred_element_type=jnp.float32)


def finish(comp_index, fragment, source_matrix, kernel, wet_points):
    bins, points = fragment.shape
    local_bins = source_matrix.shape[0]
    levels = kernel.shape[0]
    steps = 3
    tile = local_bins // steps
    return pl.pallas_call(
        finish_body,
        grid=(steps,),
        out_shape=[
            jax.ShapeDtypeStruct((local_bins, points), jnp.bfloat16),
            jax.ShapeDtypeStruct((levels, points), jnp.float32),
        ],
        in_specs=[
            pl.BlockSpec(memory_space=pltpu.SMEM),
            pl.BlockSpec((bins, points), lambda i: (0, 0)),
            pl.BlockSpec((tile, bins), lambda i: (i, 0)),
            pl.BlockSpec((levels, bins), lambda i: (0, 0)),
            pl.BlockSpec((1, points), lambda i: (0, 0)),
        ],
        out_specs=[
            pl.BlockSpec((tile, points), lambda i: (i, 0)),
            pl.BlockSpec((levels, points), lambda i: (0, 0)),
        ],
        compiler_params=pltpu.CompilerParams(vmem_limit_bytes=8 << 20),
        cost_estimate=pl.CostEstimate(
            flops=2 * bins * points * (local_bins + levels), bytes_accessed=2_500_000, transcendentals=0
        ),
        name="finish",
    )(comp_index.reshape(1), fragment, source_matrix, kernel, wet_points)


def step(spectrum, wet_mask, currents, remap_index, remap_weights, source_matrix):
    wide_index = lax.axis_index("wide")
    comp_index = lax.axis_index("comp")
    strips, wides = lax.axis_size("strip"), lax.axis_size("wide")
    comps = lax.axis_size("comp")
    local_bins, points = spectrum.shape
    groups = wides // ROWS
    group_index = wide_index // ROWS
    member = wide_index % ROWS
    share = local_bins // ROWS
    near = [[ROWS * g + i for i in range(ROWS)] for g in range(groups)]
    far = [[ROWS * g + i for g in range(groups)] for i in range(ROWS)]

    message = pack((wide_index % 16).reshape(1), spectrum.reshape(ROWS, share, points), currents)
    own = lax.all_to_all(
        message, "wide", split_axis=0, concat_axis=0, tiled=True, axis_index_groups=near
    )
    places = jnp.stack(
        [jnp.maximum(group_index - 1, 0), group_index, jnp.minimum(group_index + 1, groups - 1)]
    )
    fetched = fetch(places, remap_index, remap_weights, wet_mask)
    table = lax.all_to_all(
        unpack(own, groups),
        "wide", split_axis=0, concat_axis=0, tiled=True, axis_index_groups=far,
    )
    total = strips * wides
    upward = [(i, i + ROWS) for i in range(total - ROWS)]
    downward = [(i + ROWS, i) for i in range(total - ROWS)]
    chain = ("strip", "wide")
    bins = own[:, :share]
    below = lax.ppermute(bins, chain, upward)
    above = lax.ppermute(bins, chain, downward)
    fown = interpolate((1,), table, *fetched)
    crossing = [
        (s * wides + wides - ROWS + i, (s + 1) * wides + i) for s in range(strips - 1) for i in range(ROWS)
    ]
    fother = lax.ppermute(fown, chain, crossing + [(b, a) for a, b in crossing])
    fbeside = interpolate((0, 2), table, *fetched)
    edges = jnp.stack([group_index == 0, group_index == groups - 1]).astype(jnp.int32)

    first_bin = comp_index * local_bins + member * share
    east, north = bin_speeds(first_bin, share)
    spread = propagate(edges, below, own, above, fown, fbeside, fother, east, north)

    both = [
        [(ROWS * g + i) * comps + k for k in range(comps) for i in range(ROWS)] for g in range(groups)
    ]
    fragment = lax.all_to_all(
        spread, ("wide", "comp"), split_axis=0, concat_axis=0, tiled=True, axis_index_groups=both
    ).reshape(comps * local_bins, points)

    level_rows = LEVELS // comps
    kernel = stokes_kernel(comps * local_bins, comp_index * level_rows, level_rows)
    wet_points = lax.dynamic_slice_in_dim(wet_mask, wide_index, 1, 0).astype(jnp.float32)
    updated, stokes = finish(comp_index, fragment, source_matrix, kernel, wet_points)
    return (updated, stokes.reshape(2, level_rows, points))


def solution(mesh):
    placed = (
        P("comp", ("strip", "wide")),
        P("strip", None),
        P(None, "strip", "wide"),
        P(None, "strip"),
        P(None, "strip"),
        P("comp", None),
    )
    return jax.shard_map(
        step,
        mesh=mesh,
        in_specs=placed,
        out_specs=(P("comp", ("strip", "wide")), P(None, "comp", ("strip", "wide"))),
        check_vma=False,
    )
```

```python
import functools
import math

import jax
import jax.numpy as jnp
from jax import lax
from jax.experimental import pallas as pl
from jax.experimental.pallas import tpu as pltpu
from jax.sharding import PartitionSpec as P


NFREQ = 32
NDIR = 36
LEVELS = 32
SUBSTEPS = 4
OCEAN_ROWS = 8
OCEAN_COLS = 192
EXTRA = 16
ROWS = 4

courant = 0.45


def bin_speeds(first_bin, bin_count):
    index = first_bin + jnp.arange(bin_count, dtype=jnp.int32)
    freq_index = (index // NDIR).astype(jnp.float32)
    dir_index = (index % NDIR).astype(jnp.float32)
    group_speed = 0.35 + 0.65 * (NFREQ - 1 - freq_index) / (NFREQ - 1)
    heading = 2.0 * math.pi * (dir_index + 0.5) / NDIR
    speed_east = courant * group_speed * jnp.cos(heading)
    speed_north = courant * group_speed * jnp.sin(heading)
    return (
        jnp.broadcast_to(speed_east[:, None], (bin_count, 128)),
        jnp.broadcast_to(speed_north[:, None], (bin_count, 128)),
    )


def stokes_kernel(bin_count, first_level, level_count):
    index = jnp.arange(bin_count, dtype=jnp.int32)
    frequency = (index // NDIR + 1).astype(jnp.float32)
    heading = 2.0 * math.pi * ((index % NDIR).astype(jnp.float32) + 0.5) / NDIR
    level_index = (first_level + jnp.arange(level_count, dtype=jnp.int32)).astype(jnp.float32)
    damping = jnp.exp(-4.0 * frequency[None, :] * (level_index[:, None] + 0.5) / (NFREQ * LEVELS))
    amplitude = damping * (frequency / NFREQ)[None, :] / math.sqrt(NDIR)
    eastward = amplitude * jnp.cos(heading)[None, :]
    northward = amplitude * jnp.sin(heading)[None, :]
    return jnp.concatenate([eastward, northward], 0).astype(jnp.bfloat16)


def pack_body(place_ref, spectrum_ref, currents_ref, out_ref, local_ref, done):
    members, bins, _ = spectrum_ref.shape
    fetch_currents = pltpu.make_async_copy(currents_ref, local_ref, done.at[1])
    fetch_currents.start()
    copy = pltpu.make_async_copy(spectrum_ref, out_ref.at[:, pl.ds(0, bins), :], done.at[0])
    copy.start()
    lane = lax.broadcasted_iota(jnp.int32, (OCEAN_ROWS, 128), 1)
    diagonal = lax.broadcasted_iota(jnp.int32, (OCEAN_ROWS, OCEAN_ROWS), 0) == lax.broadcasted_iota(
        jnp.int32, (OCEAN_ROWS, OCEAN_ROWS), 1
    )
    fetch_currents.wait()
    ours = jnp.zeros((OCEAN_ROWS, 128), jnp.float32)
    for c in range(2):
        for i in range(4):
            line = jnp.broadcast_to(local_ref[c, i : i + 1, :], (OCEAN_ROWS, OCEAN_ROWS))
            column = jnp.sum(jnp.where(diagonal, line, 0.0), axis=1, keepdims=True)
            ours = jnp.where((lane & 7) == 4 * c + i, column, ours)
    ours = jnp.where((lane >> 3) == place_ref[0], ours, 0.0)
    high = ours.astype(jnp.bfloat16).astype(jnp.float32)
    rest = ours - high
    middle = rest.astype(jnp.bfloat16).astype(jnp.float32)
    low = rest - middle
    block = jnp.concatenate(
        [jnp.concatenate([high, middle], 1), jnp.concatenate([low, jnp.zeros_like(low)], 1)], 0
    ).astype(jnp.bfloat16)
    for member in range(members):
        out_ref[member, bins:, :] = block
    copy.wait()


def pack(place, spectrum, currents):
    members, bins, cols = spectrum.shape
    return pl.pallas_call(
        pack_body,
        out_shape=jax.ShapeDtypeStruct((members, bins + EXTRA, cols), jnp.bfloat16),
        in_specs=[
            pl.BlockSpec(memory_space=pltpu.SMEM),
            pl.BlockSpec(memory_space=pltpu.HBM),
            pl.BlockSpec(memory_space=pltpu.HBM),
        ],
        out_specs=pl.BlockSpec(memory_space=pltpu.VMEM),
        scratch_shapes=[
            pltpu.VMEM((2, 4, OCEAN_ROWS), jnp.float32),
            pltpu.SemaphoreType.DMA((2,)),
        ],
        cost_estimate=pl.CostEstimate(flops=100_000, bytes_accessed=700_000, transcendentals=0),
        name="pack",
    )(place, spectrum, jnp.transpose(currents, (0, 2, 1)))


def unpack_body(own_ref, out_ref):
    members = own_ref.shape[0]
    table = jnp.zeros((OCEAN_ROWS, 128), jnp.float32)
    for member in range(members):
        block = own_ref[member].astype(jnp.float32)
        upper, lower = block[:OCEAN_ROWS], block[OCEAN_ROWS:]
        table += (upper[:, :128] + upper[:, 128:]) + lower[:, :128]
    for group in range(out_ref.shape[0]):
        out_ref[group] = table


def unpack(own, groups):
    members, depth, cols = own.shape
    return pl.pallas_call(
        unpack_body,
        grid=(1,),
        out_shape=jax.ShapeDtypeStruct((groups, OCEAN_ROWS, 128), jnp.float32),
        in_specs=[pl.BlockSpec((members, EXTRA, cols), lambda i: (0, depth // EXTRA - 1, 0))],
        out_specs=pl.BlockSpec((groups, OCEAN_ROWS, 128), lambda i: (0, 0, 0)),
        compiler_params=pltpu.CompilerParams(vmem_limit_bytes=4 << 20),
        cost_estimate=pl.CostEstimate(flops=20_000, bytes_accessed=100_000, transcendentals=0),
        name="unpack",
    )(own)


def fetch_body(place_ref, index_ref, weight_ref, mask_ref, code_ref, share_ref, wet_ref):
    cells = index_ref[...]
    row_of = (cells * 5462) >> 20
    column_of = cells - row_of * OCEAN_COLS
    lane_of = ((column_of & 63) >> 2) * 8 + (column_of & 3)
    code_ref[0] = row_of * 1024 + (column_of >> 6) * 128 + lane_of
    share_ref[0] = weight_ref[...]
    upper = place_ref[pl.program_id(0)] % 2 == 1
    mask = jnp.where(upper, mask_ref[ROWS:, :], mask_ref[:ROWS, :])
    wet_ref[0] = mask.astype(jnp.float32)


def fetch(places, remap_index, remap_weights, wet_mask):
    count = places.shape[0]
    cols = wet_mask.shape[1]
    block = ROWS * cols
    return pl.pallas_call(
        fetch_body,
        grid_spec=pltpu.PrefetchScalarGridSpec(
            num_scalar_prefetch=1,
            grid=(count,),
            in_specs=[
                pl.BlockSpec((4, block), lambda i, place: (0, place[i])),
                pl.BlockSpec((4, block), lambda i, place: (0, place[i])),
                pl.BlockSpec((2 * ROWS, cols), lambda i, place: (place[i] // 2, 0)),
            ],
            out_specs=[
                pl.BlockSpec((1, 4, block), lambda i, place: (i, 0, 0)),
                pl.BlockSpec((1, 4, block), lambda i, place: (i, 0, 0)),
                pl.BlockSpec((1, ROWS, cols), lambda i, place: (i, 0, 0)),
            ],
        ),
        out_shape=[
            jax.ShapeDtypeStruct((count, 4, block), jnp.int32),
            jax.ShapeDtypeStruct((count, 4, block), jnp.float32),
            jax.ShapeDtypeStruct((count, ROWS, cols), jnp.float32),
        ],
        compiler_params=pltpu.CompilerParams(vmem_limit_bytes=4 << 20),
        cost_estimate=pl.CostEstimate(flops=100_000, bytes_accessed=300_000, transcendentals=0),
        name="fetch",
    )(places, remap_index, remap_weights, wet_mask)


def interpolate_body(blocks, gathered_ref, code_ref, share_ref, wet_ref, out_ref):
    groups = gathered_ref.shape[0]
    rows, cols = wet_ref.shape[1:]
    row_ids = lax.broadcasted_iota(jnp.int32, (OCEAN_ROWS, 128), 0)
    tables = []
    for part in range(groups // 4):
        pieces = [gathered_ref[4 * part + i] for i in range(4)]
        tables.append((pieces[0] + pieces[1]) + (pieces[2] + pieces[3]))
    for place, block in enumerate(blocks):
        base = place * 4 * rows
        for chunk in range(rows * cols // 128):
            lanes = slice(chunk * 128, chunk * 128 + 128)
            codes = code_ref[block, :, lanes]
            shares = share_ref[block, :, lanes]
            totals = [jnp.zeros((OCEAN_ROWS, 128), jnp.float32) for _ in range(2)]
            for corner in range(4):
                code_b = jnp.broadcast_to(codes[corner : corner + 1], (OCEAN_ROWS, 128))
                share_b = jnp.broadcast_to(shares[corner : corner + 1], (OCEAN_ROWS, 128))
                part_b = (code_b >> 7) & 7
                weight = jnp.where((code_b >> 10) == row_ids, share_b, 0.0)
                for c in range(2):
                    lane_b = (code_b & 127) + 4 * c
                    picked = jnp.take_along_axis(tables[0], lane_b, axis=1)
                    for part in range(1, len(tables)):
                        other = jnp.take_along_axis(tables[part], lane_b, axis=1)
                        picked = jnp.where(part_b == part, other, picked)
                    totals[c] += picked * weight
            row = chunk * 128 // cols
            spot = slice(chunk * 128 % cols, chunk * 128 % cols + 128)
            for c in range(2):
                at = base + c * rows + row
                out_ref[at : at + 1, spot] = courant * jnp.sum(totals[c], axis=0, keepdims=True)
        out_ref[base + 2 * rows : base + 3 * rows, :] = wet_ref[block]
        out_ref[base + 3 * rows : base + 4 * rows, :] = jnp.zeros((rows, cols), jnp.float32)


def interpolate(blocks, gathered, codes, shares, wet):
    count = len(blocks)
    rows, cols = wet.shape[1:]
    return pl.pallas_call(
        functools.partial(interpolate_body, blocks),
        out_shape=jax.ShapeDtypeStruct((count * 4 * rows, cols), jnp.float32),
        in_specs=[pl.BlockSpec(memory_space=pltpu.VMEM)] * 4,
        out_specs=pl.BlockSpec(memory_space=pltpu.VMEM),
        compiler_params=pltpu.CompilerParams(vmem_limit_bytes=4 << 20),
        cost_estimate=pl.CostEstimate(
            flops=2_000_000 * count, bytes_accessed=100_000 * count, transcendentals=0
        ),
        name="interpolate",
    )(gathered, codes, shares, wet)


def propagate_body(
    edge_ref, first_ref, own_ref, second_ref, fown_ref, fbeside_ref, fother_ref, east_ref, north_ref,
    out_ref, fbelow_ref, fabove_ref,
):
    rows, bins, cols = first_ref.shape
    swapped = edge_ref[2] == 1
    tile = 16
    deep = 4 * rows
    fother = fother_ref[...]
    fbelow_ref[...] = jnp.where(edge_ref[0] == 1, fother, fbeside_ref[0:deep, :])
    fabove_ref[...] = jnp.where(edge_ref[1] == 1, fother, fbeside_ref[deep:, :])

    def one_tile(t, carry):
        spot = pl.ds(pl.multiple_of(t * tile, tile), tile)
        speed_east = jnp.concatenate([east_ref[spot, :]] * (cols // 128), 1)
        speed_north = jnp.concatenate([north_ref[spot, :]] * (cols // 128), 1)
        energy, masks = [], []
        coefs = []
        for side, fields in enumerate((fbelow_ref, fown_ref, fabove_ref)):
            for row in range(rows):
                if side == 1:
                    cells = own_ref[row, spot, :].astype(jnp.float32)
                else:
                    first = first_ref[row, spot, :].astype(jnp.float32)
                    second = second_ref[row, spot, :].astype(jnp.float32)
                    cells = jnp.where(swapped == (side == 0), first, second)
                mask = fields[2 * rows + row : 2 * rows + row + 1, :]
                east = speed_east + fields[row : row + 1, :]
                north = speed_north + fields[rows + row : rows + row + 1, :]
                to_east = jnp.maximum(east, 0.0)
                to_north = jnp.maximum(north, 0.0)
                stay = (1.0 - jnp.abs(east)) - jnp.abs(north)
                coefs.append((stay, to_east, to_east - east, to_north, to_north - north))
                energy.append(cells * mask)
                masks.append(mask)
        count = 3 * rows
        for step in range(SUBSTEPS):
            low, high = step + 1, count - 1 - step
            fresh = list(energy)
            for i in range(low, high):
                stay, to_east, to_west, _, _ = coefs[i]
                moved = stay * energy[i]
                moved += pltpu.roll(to_east * energy[i], 1, 1)
                moved += pltpu.roll(to_west * energy[i], cols - 1, 1)
                moved += coefs[i - 1][3] * energy[i - 1]
                moved += coefs[i + 1][4] * energy[i + 1]
                fresh[i] = moved * masks[i]
            energy = fresh
        for row in range(rows):
            result = energy[rows + row].astype(jnp.bfloat16)
            out_ref[row, spot, :] = result
            out_ref[rows + row, spot, :] = result
        return carry

    lax.fori_loop(0, bins // tile, one_tile, 0)


def propagate(edges, first, own, second, fown, fbeside, fother, east, north):
    rows, bins, cols = first.shape
    return pl.pallas_call(
        propagate_body,
        out_shape=jax.ShapeDtypeStruct((2 * rows, bins, cols), jnp.bfloat16),
        in_specs=[pl.BlockSpec(memory_space=pltpu.SMEM)]
        + [pl.BlockSpec(memory_space=pltpu.VMEM)] * 8,
        out_specs=pl.BlockSpec(memory_space=pltpu.VMEM),
        scratch_shapes=[pltpu.VMEM((4 * rows, cols), jnp.float32)] * 2,
        compiler_params=pltpu.CompilerParams(vmem_limit_bytes=8 << 20),
        cost_estimate=pl.CostEstimate(flops=40_000_000, bytes_accessed=1_600_000, transcendentals=0),
        name="propagate",
    )(edges, first, own, second, fown, fbeside, fother, east, north)


def finish_body(comp_ref, fragment_ref, source_ref, kernel_ref, wet_ref, updated_ref, stokes_ref):
    rows = updated_ref.shape[0]
    steps = pl.num_programs(0)
    fragment = fragment_ref[...]
    source = jnp.dot(source_ref[...], fragment, preferred_element_type=jnp.float32)
    first = (comp_ref[0] * steps + pl.program_id(0)) * rows
    returned = fragment_ref[pl.ds(pl.multiple_of(first, 16), rows), :].astype(jnp.float32)
    updated_ref[...] = (wet_ref[...] * jnp.maximum(returned + source, 0.0)).astype(jnp.bfloat16)

    @pl.when(pl.program_id(0) == 0)
    def _():
        stokes_ref[...] = jnp.dot(kernel_ref[...], fragment, preferred_element_type=jnp.float32)


def finish(comp_index, fragment, source_matrix, kernel, wet_points):
    bins, points = fragment.shape
    local_bins = source_matrix.shape[0]
    levels = kernel.shape[0]
    steps = 3
    tile = local_bins // steps
    return pl.pallas_call(
        finish_body,
        grid=(steps,),
        out_shape=[
            jax.ShapeDtypeStruct((local_bins, points), jnp.bfloat16),
            jax.ShapeDtypeStruct((levels, points), jnp.float32),
        ],
        in_specs=[
            pl.BlockSpec(memory_space=pltpu.SMEM),
            pl.BlockSpec((bins, points), lambda i: (0, 0)),
            pl.BlockSpec((tile, bins), lambda i: (i, 0)),
            pl.BlockSpec((levels, bins), lambda i: (0, 0)),
            pl.BlockSpec((1, points), lambda i: (0, 0)),
        ],
        out_specs=[
            pl.BlockSpec((tile, points), lambda i: (i, 0)),
            pl.BlockSpec((levels, points), lambda i: (0, 0)),
        ],
        compiler_params=pltpu.CompilerParams(vmem_limit_bytes=8 << 20),
        cost_estimate=pl.CostEstimate(
            flops=2 * bins * points * (local_bins + levels), bytes_accessed=2_500_000, transcendentals=0
        ),
        name="finish",
    )(comp_index.reshape(1), fragment, source_matrix, kernel, wet_points)


def step(spectrum, wet_mask, currents, remap_index, remap_weights, source_matrix):
    wide_index = lax.axis_index("wide")
    comp_index = lax.axis_index("comp")
    strips, wides = lax.axis_size("strip"), lax.axis_size("wide")
    comps = lax.axis_size("comp")
    local_bins, points = spectrum.shape
    groups = wides // ROWS
    group_index = wide_index // ROWS
    member = wide_index % ROWS
    share = local_bins // ROWS
    near = [[ROWS * g + i for i in range(ROWS)] for g in range(groups)]
    far = [[ROWS * g + i for g in range(groups)] for i in range(ROWS)]

    message = pack((wide_index % 16).reshape(1), spectrum.reshape(ROWS, share, points), currents)
    own = lax.all_to_all(
        message, "wide", split_axis=0, concat_axis=0, tiled=True, axis_index_groups=near
    )
    places = jnp.stack(
        [jnp.maximum(group_index - 1, 0), group_index, jnp.minimum(group_index + 1, groups - 1)]
    )
    fetched = fetch(places, remap_index, remap_weights, wet_mask)
    table = lax.all_to_all(
        unpack(own, groups),
        "wide", split_axis=0, concat_axis=0, tiled=True, axis_index_groups=far,
    )
    total = strips * wides
    chain = ("strip", "wide")

    def swaps(start):
        pairs = [(g * ROWS + i, g * ROWS + ROWS + i) for g in range(start, total // ROWS - 1, 2) for i in range(ROWS)]
        return pairs + [(b, a) for a, b in pairs]

    bins = own[:, :share]
    first = lax.ppermute(bins, chain, swaps(0))
    second = lax.ppermute(bins, chain, swaps(1))
    fown = interpolate((1,), table, *fetched)
    crossing = [
        (s * wides + wides - ROWS + i, (s + 1) * wides + i) for s in range(strips - 1) for i in range(ROWS)
    ]
    fother = lax.ppermute(fown, chain, crossing + [(b, a) for a, b in crossing])
    fbeside = interpolate((0, 2), table, *fetched)
    chain_index = lax.axis_index("strip") * groups + group_index
    edges = jnp.stack([group_index == 0, group_index == groups - 1, chain_index % 2 == 1]).astype(jnp.int32)

    first_bin = comp_index * local_bins + member * share
    east, north = bin_speeds(first_bin, share)
    spread = propagate(edges, first, own, second, fown, fbeside, fother, east, north)

    both = [
        [(ROWS * g + i) * comps + k for k in range(comps) for i in range(ROWS)] for g in range(groups)
    ]
    fragment = lax.all_to_all(
        spread, ("wide", "comp"), split_axis=0, concat_axis=0, tiled=True, axis_index_groups=both
    ).reshape(comps * local_bins, points)

    level_rows = LEVELS // comps
    kernel = stokes_kernel(comps * local_bins, comp_index * level_rows, level_rows)
    wet_points = lax.dynamic_slice_in_dim(wet_mask, wide_index, 1, 0).astype(jnp.float32)
    updated, stokes = finish(comp_index, fragment, source_matrix, kernel, wet_points)
    return (updated, stokes.reshape(2, level_rows, points))


def solution(mesh):
    placed = (
        P("comp", ("strip", "wide")),
        P("strip", None),
        P(None, "strip", "wide"),
        P(None, "strip"),
        P(None, "strip"),
        P("comp", None),
    )
    return jax.shard_map(
        step,
        mesh=mesh,
        in_specs=placed,
        out_specs=(P("comp", ("strip", "wide")), P(None, "comp", ("strip", "wide"))),
        check_vma=False,
    )
```

```python
import functools
import math

import jax
import jax.numpy as jnp
from jax import lax
from jax.experimental import pallas as pl
from jax.experimental.pallas import tpu as pltpu
from jax.sharding import PartitionSpec as P


NFREQ = 32
NDIR = 36
LEVELS = 32
SUBSTEPS = 4
OCEAN_ROWS = 8
OCEAN_COLS = 192
EXTRA = 16
ROWS = 4

courant = 0.45


def bin_speeds(first_bin, bin_count):
    index = first_bin + jnp.arange(bin_count, dtype=jnp.int32)
    freq_index = (index // NDIR).astype(jnp.float32)
    dir_index = (index % NDIR).astype(jnp.float32)
    group_speed = 0.35 + 0.65 * (NFREQ - 1 - freq_index) / (NFREQ - 1)
    heading = 2.0 * math.pi * (dir_index + 0.5) / NDIR
    speed_east = courant * group_speed * jnp.cos(heading)
    speed_north = courant * group_speed * jnp.sin(heading)
    return (
        jnp.broadcast_to(speed_east[:, None], (bin_count, 128)),
        jnp.broadcast_to(speed_north[:, None], (bin_count, 128)),
    )


def stokes_kernel(bin_count, first_level, level_count):
    index = jnp.arange(bin_count, dtype=jnp.int32)
    frequency = (index // NDIR + 1).astype(jnp.float32)
    heading = 2.0 * math.pi * ((index % NDIR).astype(jnp.float32) + 0.5) / NDIR
    level_index = (first_level + jnp.arange(level_count, dtype=jnp.int32)).astype(jnp.float32)
    damping = jnp.exp(-4.0 * frequency[None, :] * (level_index[:, None] + 0.5) / (NFREQ * LEVELS))
    amplitude = damping * (frequency / NFREQ)[None, :] / math.sqrt(NDIR)
    eastward = amplitude * jnp.cos(heading)[None, :]
    northward = amplitude * jnp.sin(heading)[None, :]
    return jnp.concatenate([eastward, northward], 0).astype(jnp.bfloat16)


def pack_body(place_ref, spectrum_ref, currents_ref, out_ref, local_ref, done):
    members, bins, _ = spectrum_ref.shape
    fetch_currents = pltpu.make_async_copy(currents_ref, local_ref, done.at[1])
    fetch_currents.start()
    copy = pltpu.make_async_copy(spectrum_ref, out_ref.at[:, pl.ds(0, bins), :], done.at[0])
    copy.start()
    lane = lax.broadcasted_iota(jnp.int32, (OCEAN_ROWS, 128), 1)
    diagonal = lax.broadcasted_iota(jnp.int32, (OCEAN_ROWS, OCEAN_ROWS), 0) == lax.broadcasted_iota(
        jnp.int32, (OCEAN_ROWS, OCEAN_ROWS), 1
    )
    fetch_currents.wait()
    ours = jnp.zeros((OCEAN_ROWS, 128), jnp.float32)
    for c in range(2):
        for i in range(4):
            line = jnp.broadcast_to(local_ref[c, i : i + 1, :], (OCEAN_ROWS, OCEAN_ROWS))
            column = jnp.sum(jnp.where(diagonal, line, 0.0), axis=1, keepdims=True)
            ours = jnp.where((lane & 7) == 4 * c + i, column, ours)
    ours = jnp.where((lane >> 3) == place_ref[0], ours, 0.0)
    high = ours.astype(jnp.bfloat16).astype(jnp.float32)
    rest = ours - high
    middle = rest.astype(jnp.bfloat16).astype(jnp.float32)
    low = rest - middle
    block = jnp.concatenate(
        [jnp.concatenate([high, middle], 1), jnp.concatenate([low, jnp.zeros_like(low)], 1)], 0
    ).astype(jnp.bfloat16)
    for member in range(members):
        out_ref[member, bins:, :] = block
    copy.wait()


def pack(place, spectrum, currents):
    members, bins, cols = spectrum.shape
    return pl.pallas_call(
        pack_body,
        out_shape=jax.ShapeDtypeStruct((members, bins + EXTRA, cols), jnp.bfloat16),
        in_specs=[
            pl.BlockSpec(memory_space=pltpu.SMEM),
            pl.BlockSpec(memory_space=pltpu.HBM),
            pl.BlockSpec(memory_space=pltpu.HBM),
        ],
        out_specs=pl.BlockSpec(memory_space=pltpu.VMEM),
        scratch_shapes=[
            pltpu.VMEM((2, 4, OCEAN_ROWS), jnp.float32),
            pltpu.SemaphoreType.DMA((2,)),
        ],
        cost_estimate=pl.CostEstimate(flops=100_000, bytes_accessed=700_000, transcendentals=0),
        name="pack",
    )(place, spectrum, jnp.transpose(currents, (0, 2, 1)))


def unpack_body(own_ref, out_ref):
    members = own_ref.shape[0]
    table = jnp.zeros((OCEAN_ROWS, 128), jnp.float32)
    for member in range(members):
        block = own_ref[member].astype(jnp.float32)
        upper, lower = block[:OCEAN_ROWS], block[OCEAN_ROWS:]
        table += (upper[:, :128] + upper[:, 128:]) + lower[:, :128]
    for group in range(out_ref.shape[0]):
        out_ref[group] = table


def unpack(own, groups):
    members, depth, cols = own.shape
    return pl.pallas_call(
        unpack_body,
        grid=(1,),
        out_shape=jax.ShapeDtypeStruct((groups, OCEAN_ROWS, 128), jnp.float32),
        in_specs=[pl.BlockSpec((members, EXTRA, cols), lambda i: (0, depth // EXTRA - 1, 0))],
        out_specs=pl.BlockSpec((groups, OCEAN_ROWS, 128), lambda i: (0, 0, 0)),
        compiler_params=pltpu.CompilerParams(vmem_limit_bytes=4 << 20),
        cost_estimate=pl.CostEstimate(flops=20_000, bytes_accessed=100_000, transcendentals=0),
        name="unpack",
    )(own)


def fetch_body(place_ref, index_ref, weight_ref, mask_ref, code_ref, share_ref, wet_ref):
    cells = index_ref[...]
    row_of = (cells * 5462) >> 20
    column_of = cells - row_of * OCEAN_COLS
    lane_of = ((column_of & 63) >> 2) * 8 + (column_of & 3)
    code_ref[0] = row_of * 1024 + (column_of >> 6) * 128 + lane_of
    share_ref[0] = weight_ref[...]
    upper = place_ref[pl.program_id(0)] % 2 == 1
    mask = jnp.where(upper, mask_ref[ROWS:, :], mask_ref[:ROWS, :])
    wet_ref[0] = mask.astype(jnp.float32)


def fetch(places, remap_index, remap_weights, wet_mask):
    count = places.shape[0]
    cols = wet_mask.shape[1]
    block = ROWS * cols
    return pl.pallas_call(
        fetch_body,
        grid_spec=pltpu.PrefetchScalarGridSpec(
            num_scalar_prefetch=1,
            grid=(count,),
            in_specs=[
                pl.BlockSpec((4, block), lambda i, place: (0, place[i])),
                pl.BlockSpec((4, block), lambda i, place: (0, place[i])),
                pl.BlockSpec((2 * ROWS, cols), lambda i, place: (place[i] // 2, 0)),
            ],
            out_specs=[
                pl.BlockSpec((1, 4, block), lambda i, place: (i, 0, 0)),
                pl.BlockSpec((1, 4, block), lambda i, place: (i, 0, 0)),
                pl.BlockSpec((1, ROWS, cols), lambda i, place: (i, 0, 0)),
            ],
        ),
        out_shape=[
            jax.ShapeDtypeStruct((count, 4, block), jnp.int32),
            jax.ShapeDtypeStruct((count, 4, block), jnp.float32),
            jax.ShapeDtypeStruct((count, ROWS, cols), jnp.float32),
        ],
        compiler_params=pltpu.CompilerParams(vmem_limit_bytes=4 << 20),
        cost_estimate=pl.CostEstimate(flops=100_000, bytes_accessed=300_000, transcendentals=0),
        name="fetch",
    )(places, remap_index, remap_weights, wet_mask)


def interpolate_body(blocks, gathered_ref, code_ref, share_ref, wet_ref, out_ref):
    groups = gathered_ref.shape[0]
    rows, cols = wet_ref.shape[1:]
    row_ids = lax.broadcasted_iota(jnp.int32, (OCEAN_ROWS, 128), 0)
    tables = []
    for part in range(groups // 4):
        pieces = [gathered_ref[4 * part + i] for i in range(4)]
        tables.append((pieces[0] + pieces[1]) + (pieces[2] + pieces[3]))
    for place, block in enumerate(blocks):
        base = place * 4 * rows
        for chunk in range(rows * cols // 128):
            lanes = slice(chunk * 128, chunk * 128 + 128)
            codes = code_ref[block, :, lanes]
            shares = share_ref[block, :, lanes]
            totals = [jnp.zeros((OCEAN_ROWS, 128), jnp.float32) for _ in range(2)]
            for corner in range(4):
                code_b = jnp.broadcast_to(codes[corner : corner + 1], (OCEAN_ROWS, 128))
                share_b = jnp.broadcast_to(shares[corner : corner + 1], (OCEAN_ROWS, 128))
                part_b = (code_b >> 7) & 7
                weight = jnp.where((code_b >> 10) == row_ids, share_b, 0.0)
                for c in range(2):
                    lane_b = (code_b & 127) + 4 * c
                    picked = jnp.take_along_axis(tables[0], lane_b, axis=1)
                    for part in range(1, len(tables)):
                        other = jnp.take_along_axis(tables[part], lane_b, axis=1)
                        picked = jnp.where(part_b == part, other, picked)
                    totals[c] += picked * weight
            row = chunk * 128 // cols
            spot = slice(chunk * 128 % cols, chunk * 128 % cols + 128)
            for c in range(2):
                at = base + c * rows + row
                out_ref[at : at + 1, spot] = courant * jnp.sum(totals[c], axis=0, keepdims=True)
        out_ref[base + 2 * rows : base + 3 * rows, :] = wet_ref[block]
        out_ref[base + 3 * rows : base + 4 * rows, :] = jnp.zeros((rows, cols), jnp.float32)


def interpolate(blocks, gathered, codes, shares, wet):
    count = len(blocks)
    rows, cols = wet.shape[1:]
    return pl.pallas_call(
        functools.partial(interpolate_body, blocks),
        out_shape=jax.ShapeDtypeStruct((count * 4 * rows, cols), jnp.float32),
        in_specs=[pl.BlockSpec(memory_space=pltpu.VMEM)] * 4,
        out_specs=pl.BlockSpec(memory_space=pltpu.VMEM),
        compiler_params=pltpu.CompilerParams(vmem_limit_bytes=4 << 20),
        cost_estimate=pl.CostEstimate(
            flops=2_000_000 * count, bytes_accessed=100_000 * count, transcendentals=0
        ),
        name="interpolate",
    )(gathered, codes, shares, wet)


def propagate_body(
    edge_ref, first_ref, own_ref, second_ref, fields_ref, fother_ref, east_ref, north_ref,
    out_ref, fbelow_ref, fabove_ref,
):
    rows, bins, _ = first_ref.shape
    deep = 4 * rows
    fother = fother_ref[...]
    fbelow_ref[...] = jnp.where(edge_ref[0] == 1, fother, fields_ref[0:deep, :])
    fabove_ref[...] = jnp.where(edge_ref[1] == 1, fother, fields_ref[2 * deep :, :])
    fields = (fbelow_ref, fields_ref.at[deep : 2 * deep, :], fabove_ref)

    @pl.when(edge_ref[2] == 1)
    def _():
        substeps((first_ref, own_ref, second_ref), fields, east_ref, north_ref, out_ref, bins)

    @pl.when(edge_ref[2] != 1)
    def _():
        substeps((second_ref, own_ref, first_ref), fields, east_ref, north_ref, out_ref, bins)


def substeps(sources, all_fields, east_ref, north_ref, out_ref, bins):
    rows, _, cols = sources[1].shape
    tile = 16

    def one_tile(t, carry):
        spot = pl.ds(pl.multiple_of(t * tile, tile), tile)
        speed_east = jnp.concatenate([east_ref[spot, :]] * (cols // 128), 1)
        speed_north = jnp.concatenate([north_ref[spot, :]] * (cols // 128), 1)
        energy, masks = [], []
        coefs = []
        for source, fields in zip(sources, all_fields):
            for row in range(rows):
                mask = fields[2 * rows + row : 2 * rows + row + 1, :]
                east = speed_east + fields[row : row + 1, :]
                north = speed_north + fields[rows + row : rows + row + 1, :]
                to_east = jnp.maximum(east, 0.0)
                to_north = jnp.maximum(north, 0.0)
                stay = (1.0 - jnp.abs(east)) - jnp.abs(north)
                coefs.append((stay, to_east, to_east - east, to_north, to_north - north))
                energy.append(source[row, spot, :].astype(jnp.float32) * mask)
                masks.append(mask)
        count = 3 * rows
        for step in range(SUBSTEPS):
            low, high = step + 1, count - 1 - step
            fresh = list(energy)
            for i in range(low, high):
                stay, to_east, to_west, _, _ = coefs[i]
                moved = stay * energy[i]
                moved += pltpu.roll(to_east * energy[i], 1, 1)
                moved += pltpu.roll(to_west * energy[i], cols - 1, 1)
                moved += coefs[i - 1][3] * energy[i - 1]
                moved += coefs[i + 1][4] * energy[i + 1]
                fresh[i] = moved * masks[i]
            energy = fresh
        for row in range(rows):
            result = energy[rows + row].astype(jnp.bfloat16)
            out_ref[row, spot, :] = result
            out_ref[rows + row, spot, :] = result
        return carry

    lax.fori_loop(0, bins // tile, one_tile, 0)


def propagate(edges, first, own, second, fields, fother, east, north):
    rows, bins, cols = first.shape
    return pl.pallas_call(
        propagate_body,
        out_shape=jax.ShapeDtypeStruct((2 * rows, bins, cols), jnp.bfloat16),
        in_specs=[pl.BlockSpec(memory_space=pltpu.SMEM)]
        + [pl.BlockSpec(memory_space=pltpu.VMEM)] * 7,
        out_specs=pl.BlockSpec(memory_space=pltpu.VMEM),
        scratch_shapes=[pltpu.VMEM((4 * rows, cols), jnp.float32)] * 2,
        compiler_params=pltpu.CompilerParams(vmem_limit_bytes=8 << 20),
        cost_estimate=pl.CostEstimate(flops=40_000_000, bytes_accessed=1_600_000, transcendentals=0),
        name="propagate",
    )(edges, first, own, second, fields, fother, east, north)


def finish_body(comp_ref, fragment_ref, source_ref, kernel_ref, wet_ref, updated_ref, stokes_ref):
    rows = updated_ref.shape[0]
    steps = pl.num_programs(0)
    fragment = fragment_ref[...]
    source = jnp.dot(source_ref[...], fragment, preferred_element_type=jnp.float32)
    first = (comp_ref[0] * steps + pl.program_id(0)) * rows
    returned = fragment_ref[pl.ds(pl.multiple_of(first, 16), rows), :].astype(jnp.float32)
    updated_ref[...] = (wet_ref[...] * jnp.maximum(returned + source, 0.0)).astype(jnp.bfloat16)

    @pl.when(pl.program_id(0) == 0)
    def _():
        stokes_ref[...] = jnp.dot(kernel_ref[...], fragment, preferred_element_type=jnp.float32)


def finish(comp_index, fragment, source_matrix, kernel, wet_points):
    bins, points = fragment.shape
    local_bins = source_matrix.shape[0]
    levels = kernel.shape[0]
    steps = 1
    tile = local_bins // steps
    return pl.pallas_call(
        finish_body,
        grid=(steps,),
        out_shape=[
            jax.ShapeDtypeStruct((local_bins, points), jnp.bfloat16),
            jax.ShapeDtypeStruct((levels, points), jnp.float32),
        ],
        in_specs=[
            pl.BlockSpec(memory_space=pltpu.SMEM),
            pl.BlockSpec((bins, points), lambda i: (0, 0)),
            pl.BlockSpec((tile, bins), lambda i: (i, 0)),
            pl.BlockSpec((levels, bins), lambda i: (0, 0)),
            pl.BlockSpec((1, points), lambda i: (0, 0)),
        ],
        out_specs=[
            pl.BlockSpec((tile, points), lambda i: (i, 0)),
            pl.BlockSpec((levels, points), lambda i: (0, 0)),
        ],
        compiler_params=pltpu.CompilerParams(vmem_limit_bytes=8 << 20),
        cost_estimate=pl.CostEstimate(
            flops=2 * bins * points * (local_bins + levels), bytes_accessed=2_500_000, transcendentals=0
        ),
        name="finish",
    )(comp_index.reshape(1), fragment, source_matrix, kernel, wet_points)


def step(spectrum, wet_mask, currents, remap_index, remap_weights, source_matrix):
    wide_index = lax.axis_index("wide")
    comp_index = lax.axis_index("comp")
    strips, wides = lax.axis_size("strip"), lax.axis_size("wide")
    comps = lax.axis_size("comp")
    local_bins, points = spectrum.shape
    groups = wides // ROWS
    group_index = wide_index // ROWS
    member = wide_index % ROWS
    share = local_bins // ROWS
    near = [[ROWS * g + i for i in range(ROWS)] for g in range(groups)]
    far = [[ROWS * g + i for g in range(groups)] for i in range(ROWS)]

    message = pack((wide_index % 16).reshape(1), spectrum.reshape(ROWS, share, points), currents)
    own = lax.all_to_all(
        message, "wide", split_axis=0, concat_axis=0, tiled=True, axis_index_groups=near
    )
    lowest, highest = group_index == 0, group_index == groups - 1
    places = jnp.stack(
        [
            jnp.maximum(group_index - 1, 0),
            group_index,
            jnp.minimum(group_index + 1, groups - 1),
            jnp.where(lowest, groups - 1, 0),
        ]
    )
    fetched = fetch(places, remap_index, remap_weights, wet_mask)
    table = lax.all_to_all(
        unpack(own, groups),
        "wide", split_axis=0, concat_axis=0, tiled=True, axis_index_groups=far,
    )
    total = strips * wides
    chain = ("strip", "wide")

    def swaps(start):
        pairs = [(g * ROWS + i, g * ROWS + ROWS + i) for g in range(start, total // ROWS - 1, 2) for i in range(ROWS)]
        return pairs + [(b, a) for a, b in pairs]

    bins = own[:, :share]
    first = lax.ppermute(bins, chain, swaps(0))
    second = lax.ppermute(bins, chain, swaps(1))
    fedge = interpolate((3,), table, *fetched)
    edge_moves = []
    for s in range(strips - 1):
        for i in range(ROWS):
            last = wides - ROWS + i
            edge_moves += [(s * wides + i, (s + 1) * wides + i), ((s + 1) * wides + last, s * wides + last)]
    fother = lax.ppermute(fedge, chain, edge_moves)
    fields = interpolate((0, 1, 2), table, *fetched)
    chain_index = lax.axis_index("strip") * groups + group_index
    edges = jnp.stack([lowest, highest, chain_index % 2 == 1]).astype(jnp.int32)

    first_bin = comp_index * local_bins + member * share
    east, north = bin_speeds(first_bin, share)
    spread = propagate(edges, first, own, second, fields, fother, east, north)

    both = [
        [(ROWS * g + i) * comps + k for k in range(comps) for i in range(ROWS)] for g in range(groups)
    ]
    fragment = lax.all_to_all(
        spread, ("wide", "comp"), split_axis=0, concat_axis=0, tiled=True, axis_index_groups=both
    ).reshape(comps * local_bins, points)

    level_rows = LEVELS // comps
    kernel = stokes_kernel(comps * local_bins, comp_index * level_rows, level_rows)
    wet_points = lax.dynamic_slice_in_dim(wet_mask, wide_index, 1, 0).astype(jnp.float32)
    updated, stokes = finish(comp_index, fragment, source_matrix, kernel, wet_points)
    return (updated, stokes.reshape(2, level_rows, points))


def solution(mesh):
    placed = (
        P("comp", ("strip", "wide")),
        P("strip", None),
        P(None, "strip", "wide"),
        P(None, "strip"),
        P(None, "strip"),
        P("comp", None),
    )
    return jax.shard_map(
        step,
        mesh=mesh,
        in_specs=placed,
        out_specs=(P("comp", ("strip", "wide")), P(None, "comp", ("strip", "wide"))),
        check_vma=False,
    )
```

```python
import functools
import math

import jax
import jax.numpy as jnp
from jax import lax
from jax.experimental import pallas as pl
from jax.experimental.pallas import tpu as pltpu
from jax.sharding import PartitionSpec as P


NFREQ = 32
NDIR = 36
LEVELS = 32
SUBSTEPS = 4
OCEAN_ROWS = 8
OCEAN_COLS = 192
EXTRA = 16
ROWS = 4

courant = 0.45


def bin_speeds(first_bin, bin_count):
    index = first_bin + jnp.arange(bin_count, dtype=jnp.int32)
    freq_index = (index // NDIR).astype(jnp.float32)
    dir_index = (index % NDIR).astype(jnp.float32)
    group_speed = 0.35 + 0.65 * (NFREQ - 1 - freq_index) / (NFREQ - 1)
    heading = 2.0 * math.pi * (dir_index + 0.5) / NDIR
    speed_east = courant * group_speed * jnp.cos(heading)
    speed_north = courant * group_speed * jnp.sin(heading)
    return (
        jnp.broadcast_to(speed_east[:, None], (bin_count, 128)),
        jnp.broadcast_to(speed_north[:, None], (bin_count, 128)),
    )


def stokes_kernel(bin_count, first_level, level_count):
    index = jnp.arange(bin_count, dtype=jnp.int32)
    frequency = (index // NDIR + 1).astype(jnp.float32)
    heading = 2.0 * math.pi * ((index % NDIR).astype(jnp.float32) + 0.5) / NDIR
    level_index = (first_level + jnp.arange(level_count, dtype=jnp.int32)).astype(jnp.float32)
    damping = jnp.exp(-4.0 * frequency[None, :] * (level_index[:, None] + 0.5) / (NFREQ * LEVELS))
    amplitude = damping * (frequency / NFREQ)[None, :] / math.sqrt(NDIR)
    eastward = amplitude * jnp.cos(heading)[None, :]
    northward = amplitude * jnp.sin(heading)[None, :]
    return jnp.concatenate([eastward, northward], 0).astype(jnp.bfloat16)


def pack_body(place_ref, spectrum_ref, currents_ref, out_ref, local_ref, done):
    members, bins, _ = spectrum_ref.shape
    fetch_currents = pltpu.make_async_copy(currents_ref, local_ref, done.at[1])
    fetch_currents.start()
    copy = pltpu.make_async_copy(spectrum_ref, out_ref.at[:, pl.ds(0, bins), :], done.at[0])
    copy.start()
    lane = lax.broadcasted_iota(jnp.int32, (OCEAN_ROWS, 128), 1)
    diagonal = lax.broadcasted_iota(jnp.int32, (OCEAN_ROWS, OCEAN_ROWS), 0) == lax.broadcasted_iota(
        jnp.int32, (OCEAN_ROWS, OCEAN_ROWS), 1
    )
    fetch_currents.wait()
    ours = jnp.zeros((OCEAN_ROWS, 128), jnp.float32)
    for c in range(2):
        for i in range(4):
            line = jnp.broadcast_to(local_ref[c, i : i + 1, :], (OCEAN_ROWS, OCEAN_ROWS))
            column = jnp.sum(jnp.where(diagonal, line, 0.0), axis=1, keepdims=True)
            ours = jnp.where((lane & 7) == 4 * c + i, column, ours)
    ours = jnp.where((lane >> 3) == place_ref[0], ours, 0.0)
    high = ours.astype(jnp.bfloat16).astype(jnp.float32)
    rest = ours - high
    middle = rest.astype(jnp.bfloat16).astype(jnp.float32)
    low = rest - middle
    block = jnp.concatenate(
        [jnp.concatenate([high, middle], 1), jnp.concatenate([low, jnp.zeros_like(low)], 1)], 0
    ).astype(jnp.bfloat16)
    for member in range(members):
        out_ref[member, bins:, :] = block
    copy.wait()


def pack(place, spectrum, currents):
    members, bins, cols = spectrum.shape
    return pl.pallas_call(
        pack_body,
        out_shape=jax.ShapeDtypeStruct((members, bins + EXTRA, cols), jnp.bfloat16),
        in_specs=[
            pl.BlockSpec(memory_space=pltpu.SMEM),
            pl.BlockSpec(memory_space=pltpu.HBM),
            pl.BlockSpec(memory_space=pltpu.HBM),
        ],
        out_specs=pl.BlockSpec(memory_space=pltpu.VMEM),
        scratch_shapes=[
            pltpu.VMEM((2, 4, OCEAN_ROWS), jnp.float32),
            pltpu.SemaphoreType.DMA((2,)),
        ],
        cost_estimate=pl.CostEstimate(flops=100_000, bytes_accessed=700_000, transcendentals=0),
        name="pack",
    )(place, spectrum, jnp.transpose(currents, (0, 2, 1)))


def unpack_body(own_ref, out_ref):
    members = own_ref.shape[0]
    table = jnp.zeros((OCEAN_ROWS, 128), jnp.float32)
    for member in range(members):
        block = own_ref[member].astype(jnp.float32)
        upper, lower = block[:OCEAN_ROWS], block[OCEAN_ROWS:]
        table += (upper[:, :128] + upper[:, 128:]) + lower[:, :128]
    for group in range(out_ref.shape[0]):
        out_ref[group] = table


def unpack(own, groups):
    members, depth, cols = own.shape
    return pl.pallas_call(
        unpack_body,
        grid=(1,),
        out_shape=jax.ShapeDtypeStruct((groups, OCEAN_ROWS, 128), jnp.float32),
        in_specs=[pl.BlockSpec((members, EXTRA, cols), lambda i: (0, depth // EXTRA - 1, 0))],
        out_specs=pl.BlockSpec((groups, OCEAN_ROWS, 128), lambda i: (0, 0, 0)),
        compiler_params=pltpu.CompilerParams(vmem_limit_bytes=4 << 20),
        cost_estimate=pl.CostEstimate(flops=20_000, bytes_accessed=100_000, transcendentals=0),
        name="unpack",
    )(own)


def fetch_body(place_ref, index_ref, weight_ref, mask_ref, code_ref, share_ref, wet_ref):
    cells = index_ref[...]
    row_of = (cells * 5462) >> 20
    column_of = cells - row_of * OCEAN_COLS
    lane_of = ((column_of & 63) >> 2) * 8 + (column_of & 3)
    code_ref[0] = row_of * 1024 + (column_of >> 6) * 128 + lane_of
    share_ref[0] = weight_ref[...]
    upper = place_ref[pl.program_id(0)] % 2 == 1
    mask = jnp.where(upper, mask_ref[ROWS:, :], mask_ref[:ROWS, :])
    wet_ref[0] = mask.astype(jnp.float32)


def fetch(places, remap_index, remap_weights, wet_mask):
    count = places.shape[0]
    cols = wet_mask.shape[1]
    block = ROWS * cols
    return pl.pallas_call(
        fetch_body,
        grid_spec=pltpu.PrefetchScalarGridSpec(
            num_scalar_prefetch=1,
            grid=(count,),
            in_specs=[
                pl.BlockSpec((4, block), lambda i, place: (0, place[i])),
                pl.BlockSpec((4, block), lambda i, place: (0, place[i])),
                pl.BlockSpec((2 * ROWS, cols), lambda i, place: (place[i] // 2, 0)),
            ],
            out_specs=[
                pl.BlockSpec((1, 4, block), lambda i, place: (i, 0, 0)),
                pl.BlockSpec((1, 4, block), lambda i, place: (i, 0, 0)),
                pl.BlockSpec((1, ROWS, cols), lambda i, place: (i, 0, 0)),
            ],
        ),
        out_shape=[
            jax.ShapeDtypeStruct((count, 4, block), jnp.int32),
            jax.ShapeDtypeStruct((count, 4, block), jnp.float32),
            jax.ShapeDtypeStruct((count, ROWS, cols), jnp.float32),
        ],
        compiler_params=pltpu.CompilerParams(vmem_limit_bytes=4 << 20),
        cost_estimate=pl.CostEstimate(flops=100_000, bytes_accessed=300_000, transcendentals=0),
        name="fetch",
    )(places, remap_index, remap_weights, wet_mask)


def visit_order(groups):
    half = groups // 2
    return [g // 2 + (g % 2) * half for g in range(groups)] if groups % 2 == 0 else list(range(groups))


def interpolate_body(blocks, gathered_ref, code_ref, share_ref, wet_ref, out_ref):
    groups = gathered_ref.shape[0]
    rows, cols = wet_ref.shape[1:]
    row_ids = lax.broadcasted_iota(jnp.int32, (OCEAN_ROWS, 128), 0)
    order = visit_order(groups)
    tables = []
    for part in range(groups // 4):
        pieces = [gathered_ref[order.index(4 * part + i)] for i in range(4)]
        tables.append((pieces[0] + pieces[1]) + (pieces[2] + pieces[3]))
    for place, block in enumerate(blocks):
        base = place * 4 * rows
        for chunk in range(rows * cols // 128):
            lanes = slice(chunk * 128, chunk * 128 + 128)
            codes = code_ref[block, :, lanes]
            shares = share_ref[block, :, lanes]
            totals = [jnp.zeros((OCEAN_ROWS, 128), jnp.float32) for _ in range(2)]
            for corner in range(4):
                code_b = jnp.broadcast_to(codes[corner : corner + 1], (OCEAN_ROWS, 128))
                share_b = jnp.broadcast_to(shares[corner : corner + 1], (OCEAN_ROWS, 128))
                part_b = (code_b >> 7) & 7
                weight = jnp.where((code_b >> 10) == row_ids, share_b, 0.0)
                for c in range(2):
                    lane_b = (code_b & 127) + 4 * c
                    picked = jnp.take_along_axis(tables[0], lane_b, axis=1)
                    for part in range(1, len(tables)):
                        other = jnp.take_along_axis(tables[part], lane_b, axis=1)
                        picked = jnp.where(part_b == part, other, picked)
                    totals[c] += picked * weight
            row = chunk * 128 // cols
            spot = slice(chunk * 128 % cols, chunk * 128 % cols + 128)
            for c in range(2):
                at = base + c * rows + row
                out_ref[at : at + 1, spot] = courant * jnp.sum(totals[c], axis=0, keepdims=True)
        out_ref[base + 2 * rows : base + 3 * rows, :] = wet_ref[block]
        out_ref[base + 3 * rows : base + 4 * rows, :] = jnp.zeros((rows, cols), jnp.float32)


def interpolate(blocks, gathered, codes, shares, wet):
    count = len(blocks)
    rows, cols = wet.shape[1:]
    return pl.pallas_call(
        functools.partial(interpolate_body, blocks),
        out_shape=jax.ShapeDtypeStruct((count * 4 * rows, cols), jnp.float32),
        in_specs=[pl.BlockSpec(memory_space=pltpu.VMEM)] * 4,
        out_specs=pl.BlockSpec(memory_space=pltpu.VMEM),
        compiler_params=pltpu.CompilerParams(vmem_limit_bytes=4 << 20),
        cost_estimate=pl.CostEstimate(
            flops=2_000_000 * count, bytes_accessed=100_000 * count, transcendentals=0
        ),
        name="interpolate",
    )(gathered, codes, shares, wet)


def propagate_body(
    edge_ref, first_ref, own_ref, second_ref, fields_ref, fother_ref, east_ref, north_ref,
    out_ref, fbelow_ref, fabove_ref, ready_ref, done,
):
    rows, _, _ = first_ref.shape
    deep = 4 * rows
    fother = fother_ref[...]
    fbelow_ref[...] = jnp.where(edge_ref[0] == 1, fother, fields_ref[0:deep, :])
    fabove_ref[...] = jnp.where(edge_ref[1] == 1, fother, fields_ref[2 * deep :, :])
    fields = (fbelow_ref, fields_ref.at[deep : 2 * deep, :], fabove_ref)

    @pl.when(edge_ref[2] == 1)
    def _():
        substeps((first_ref, own_ref, second_ref), fields, east_ref, north_ref, out_ref, ready_ref, done)

    @pl.when(edge_ref[2] != 1)
    def _():
        substeps((second_ref, own_ref, first_ref), fields, east_ref, north_ref, out_ref, ready_ref, done)


def substeps(sources, all_fields, east_ref, north_ref, out_ref, ready_ref, done):
    rows, _, cols = sources[1].shape
    bins = out_ref.shape[1]
    tile = 16

    def copy_out(t):
        spot = pl.ds(pl.multiple_of(t * tile, tile), tile)
        return pltpu.make_async_copy(ready_ref.at[:, spot, :], out_ref.at[:, spot, :], done.at[t])

    def one_tile(t, carry):
        spot = pl.ds(pl.multiple_of(t * tile, tile), tile)
        speed_east = jnp.concatenate([east_ref[spot, :]] * (cols // 128), 1)
        speed_north = jnp.concatenate([north_ref[spot, :]] * (cols // 128), 1)
        energy, masks = [], []
        coefs = []
        for source, fields in zip(sources, all_fields):
            for row in range(rows):
                mask = fields[2 * rows + row : 2 * rows + row + 1, :]
                east = speed_east + fields[row : row + 1, :]
                north = speed_north + fields[rows + row : rows + row + 1, :]
                to_east = jnp.maximum(east, 0.0)
                to_north = jnp.maximum(north, 0.0)
                stay = (1.0 - jnp.abs(east)) - jnp.abs(north)
                coefs.append((stay, to_east, to_east - east, to_north, to_north - north))
                energy.append(source[row, spot, :].astype(jnp.float32) * mask)
                masks.append(mask)
        count = 3 * rows
        for step in range(SUBSTEPS):
            low, high = step + 1, count - 1 - step
            fresh = list(energy)
            for i in range(low, high):
                stay, to_east, to_west, _, _ = coefs[i]
                moved = stay * energy[i]
                moved += pltpu.roll(to_east * energy[i], 1, 1)
                moved += pltpu.roll(to_west * energy[i], cols - 1, 1)
                moved += coefs[i - 1][3] * energy[i - 1]
                moved += coefs[i + 1][4] * energy[i + 1]
                fresh[i] = moved * masks[i]
            energy = fresh
        for row in range(rows):
            result = energy[rows + row].astype(jnp.bfloat16)
            ready_ref[row, spot, :] = result
            ready_ref[rows + row, spot, :] = result
        copy_out(t).start()
        return carry

    lax.fori_loop(0, bins // tile, one_tile, 0)
    for t in range(bins // tile):
        copy_out(t).wait()


def propagate(edges, first, own, second, fields, fother, east, north):
    rows, bins, cols = first.shape
    return pl.pallas_call(
        propagate_body,
        out_shape=jax.ShapeDtypeStruct((2 * rows, bins, cols), jnp.bfloat16),
        in_specs=[pl.BlockSpec(memory_space=pltpu.SMEM)]
        + [pl.BlockSpec(memory_space=pltpu.VMEM)] * 7,
        out_specs=pl.BlockSpec(memory_space=pltpu.HBM),
        scratch_shapes=[pltpu.VMEM((4 * rows, cols), jnp.float32)] * 2
        + [
            pltpu.VMEM((2 * rows, bins, cols), jnp.bfloat16),
            pltpu.SemaphoreType.DMA((bins // 16,)),
        ],
        compiler_params=pltpu.CompilerParams(vmem_limit_bytes=8 << 20),
        cost_estimate=pl.CostEstimate(flops=40_000_000, bytes_accessed=1_600_000, transcendentals=0),
        name="propagate",
    )(edges, first, own, second, fields, fother, east, north)


def finish_body(
    comp_ref, fragment_ref, source_ref, kernel_ref, wet_ref, updated_ref, stokes_ref, new_ref, drift_ref, done
):
    rows = updated_ref.shape[0]
    parts = 4
    tile = rows // parts
    fragment = fragment_ref[...]
    copies = []
    for part in range(parts):
        spot = slice(part * tile, part * tile + tile)
        source = jnp.dot(source_ref[spot, :], fragment, preferred_element_type=jnp.float32)
        first = pl.multiple_of(comp_ref[0] * rows + part * tile, 16)
        returned = fragment_ref[pl.ds(first, tile), :].astype(jnp.float32)
        new_ref[spot, :] = (wet_ref[...] * jnp.maximum(returned + source, 0.0)).astype(jnp.bfloat16)
        copies.append(
            pltpu.make_async_copy(
                new_ref.at[pl.ds(part * tile, tile), :], updated_ref.at[pl.ds(part * tile, tile), :], done.at[part]
            )
        )
        copies[-1].start()
        if part == parts - 2:
            drift_ref[...] = jnp.dot(kernel_ref[...], fragment, preferred_element_type=jnp.float32)
            copies.append(pltpu.make_async_copy(drift_ref, stokes_ref, done.at[parts]))
            copies[-1].start()
    for copy in copies:
        copy.wait()


def finish(comp_index, fragment, source_matrix, kernel, wet_points):
    bins, points = fragment.shape
    local_bins = source_matrix.shape[0]
    levels = kernel.shape[0]
    return pl.pallas_call(
        finish_body,
        out_shape=[
            jax.ShapeDtypeStruct((local_bins, points), jnp.bfloat16),
            jax.ShapeDtypeStruct((levels, points), jnp.float32),
        ],
        in_specs=[pl.BlockSpec(memory_space=pltpu.SMEM)]
        + [pl.BlockSpec(memory_space=pltpu.VMEM)] * 4,
        out_specs=[pl.BlockSpec(memory_space=pltpu.HBM)] * 2,
        scratch_shapes=[
            pltpu.VMEM((local_bins, points), jnp.bfloat16),
            pltpu.VMEM((levels, points), jnp.float32),
            pltpu.SemaphoreType.DMA((5,)),
        ],
        compiler_params=pltpu.CompilerParams(vmem_limit_bytes=8 << 20),
        cost_estimate=pl.CostEstimate(
            flops=2 * bins * points * (local_bins + levels), bytes_accessed=2_500_000, transcendentals=0
        ),
        name="finish",
    )(comp_index.reshape(1), fragment, source_matrix, kernel, wet_points)


def step(spectrum, wet_mask, currents, remap_index, remap_weights, source_matrix):
    wide_index = lax.axis_index("wide")
    comp_index = lax.axis_index("comp")
    strips, wides = lax.axis_size("strip"), lax.axis_size("wide")
    comps = lax.axis_size("comp")
    local_bins, points = spectrum.shape
    groups = wides // ROWS
    group_index = wide_index // ROWS
    member = wide_index % ROWS
    share = local_bins // ROWS
    near = [[ROWS * g + i for i in range(ROWS)] for g in range(groups)]
    far = [[ROWS * g + i for g in visit_order(groups)] for i in range(ROWS)]

    message = pack((wide_index % 16).reshape(1), spectrum.reshape(ROWS, share, points), currents)
    own = lax.all_to_all(
        message, "wide", split_axis=0, concat_axis=0, tiled=True, axis_index_groups=near
    )
    lowest, highest = group_index == 0, group_index == groups - 1
    places = jnp.stack(
        [
            jnp.maximum(group_index - 1, 0),
            group_index,
            jnp.minimum(group_index + 1, groups - 1),
            jnp.where(lowest, groups - 1, 0),
        ]
    )
    fetched = fetch(places, remap_index, remap_weights, wet_mask)
    table = lax.all_to_all(
        unpack(own, groups),
        "wide", split_axis=0, concat_axis=0, tiled=True, axis_index_groups=far,
    )
    total = strips * wides
    chain = ("strip", "wide")

    def swaps(start):
        pairs = [(g * ROWS + i, g * ROWS + ROWS + i) for g in range(start, total // ROWS - 1, 2) for i in range(ROWS)]
        return pairs + [(b, a) for a, b in pairs]

    bins = own[:, :share]
    first = lax.ppermute(bins, chain, swaps(0))
    second = lax.ppermute(bins, chain, swaps(1))
    fedge = interpolate((3,), table, *fetched)
    edge_moves = []
    for s in range(strips - 1):
        for i in range(ROWS):
            last = wides - ROWS + i
            edge_moves += [(s * wides + i, (s + 1) * wides + i), ((s + 1) * wides + last, s * wides + last)]
    fother = lax.ppermute(fedge, chain, edge_moves)
    fields = interpolate((0, 1, 2), table, *fetched)
    chain_index = lax.axis_index("strip") * groups + group_index
    edges = jnp.stack([lowest, highest, chain_index % 2 == 1]).astype(jnp.int32)

    first_bin = comp_index * local_bins + member * share
    east, north = bin_speeds(first_bin, share)
    spread = propagate(edges, first, own, second, fields, fother, east, north)

    both = [
        [(ROWS * g + i) * comps + k for k in range(comps) for i in range(ROWS)] for g in range(groups)
    ]
    fragment = lax.all_to_all(
        spread, ("wide", "comp"), split_axis=0, concat_axis=0, tiled=True, axis_index_groups=both
    ).reshape(comps * local_bins, points)

    level_rows = LEVELS // comps
    kernel = stokes_kernel(comps * local_bins, comp_index * level_rows, level_rows)
    wet_points = lax.dynamic_slice_in_dim(wet_mask, wide_index, 1, 0).astype(jnp.float32)
    updated, stokes = finish(comp_index, fragment, source_matrix, kernel, wet_points)
    return (updated, stokes.reshape(2, level_rows, points))


def solution(mesh):
    placed = (
        P("comp", ("strip", "wide")),
        P("strip", None),
        P(None, "strip", "wide"),
        P(None, "strip"),
        P(None, "strip"),
        P("comp", None),
    )
    return jax.shard_map(
        step,
        mesh=mesh,
        in_specs=placed,
        out_specs=(P("comp", ("strip", "wide")), P(None, "comp", ("strip", "wide"))),
        check_vma=False,
    )
```
